128 devices in a mesh: seq: 8 (over x, core), rows: 16 (over z, y).
Axes of the slice: x: 4, y: 4, z: 4, core: 2. Of those that a mesh axis runs over, the one named last changes fastest.
Arguments:
- hidden: bfloat16 [16, 1024, 2560], P('rows', 'seq'), may hold values from -6 to 6
- row_ids: int32 [16, 1024, 8], P('rows', 'seq'), may hold values from 0 to 524287, as said below
- table: bfloat16 [524288, 128], P(('seq', 'rows')), may hold values from -6 to 6
- key_weight: bfloat16 [1024, 2560], replicated, may hold values from -0.1875 to 0.1875
- value_weight: bfloat16 [1024, 2560], replicated, may hold values from -0.1875 to 0.1875
- hidden_gain: float32 [2560], replicated, may hold values from 0.1 to 1.9
- key_gain: float32 [2560], replicated, may hold values from 0.1 to 1.9
- conv_gain: float32 [2560], replicated, may hold values from 0.1 to 1.9
- conv_kernel: float32 [4, 2560], replicated, may hold values from -3 to 3
- cotangent: bfloat16 [16, 1024, 2560], P('rows', 'seq'), may hold values from -6 to 6
Outputs:
- mixed: bfloat16 [16, 1024, 2560], P('rows', 'seq')
- hidden_grad: bfloat16 [16, 1024, 2560], P('rows', 'seq')
- table_grad: float32 [524288, 128], P(('seq', 'rows'))
The draws below stay inside these ranges and needn't reach their ends.
Inputs may be any that keep to these rules, and one draw needn't show every extreme that they name: `row_ids`: row r is held by device r // 4096 of seq+rows. Of the 1024 ids of one device, at most 24 fall on one owner, and in every draw some owners get exactly 24 from every device.
All inputs are finite; a program needn't handle non-finite values.
Results may differ from the reference program's by a relative error of at most 0.0029.
Values may be sent and summed in bfloat16 or wider, within the bound.
No kernel may reach another device: no remote copies, remote signals or barrier semaphores. Data moves between devices by JAX's collectives and lax.ppermute only.
A program may use at most 64 MiB of HBM per device.

```python
import jax
import jax.numpy as jnp
from jax import lax

D = 2560
RW = 128
KW = 4
TOK_DEV = 128
R_DEV = 4096
LOOK = 8
MEM = 1024
BATCH = 16
LENGTH = 1024
TABLE_ROWS = 524288
N_SEQ = 8
N_ROWS = 16
DEVICES = 128


def draw_row_ids(key, part):
    request_count = TOK_DEV * LOOK
    capacity = 3 * request_count // DEVICES
    ranking_key, source_key = jax.random.split(key)
    ranking = jax.random.permutation(ranking_key, DEVICES).astype(jnp.int32)
    global_rank = jnp.zeros((DEVICES,), jnp.int32).at[ranking].set(jnp.arange(DEVICES, dtype=jnp.int32))

    def one_source(source):
        key_hot, key_turn, key_place, key_local = jax.random.split(source, 4)
        hot_count = jax.random.randint(key_hot, (), 2, 5, dtype=jnp.int32)
        remaining = request_count - hot_count * capacity
        cold_owners = DEVICES - hot_count
        base_load = remaining // cold_owners
        extra_owners = remaining - base_load * cold_owners
        turn_offset = jax.random.randint(key_turn, (), 0, DEVICES, dtype=jnp.int32)
        rotation = (global_rank - hot_count + turn_offset) % cold_owners
        counts = jnp.where(global_rank < hot_count, capacity, base_load + (rotation < extra_owners).astype(jnp.int32))
        bound_sums = jnp.cumsum(counts).astype(jnp.int32)
        owners_of = jnp.searchsorted(bound_sums, jnp.arange(request_count, dtype=jnp.int32), side='right').astype(jnp.int32)
        owners_of = owners_of[jax.random.permutation(key_place, request_count)]
        local_rows = jax.random.randint(key_local, (request_count,), 0, R_DEV, dtype=jnp.int32)
        return (owners_of * R_DEV + local_rows).reshape(TOK_DEV, LOOK)
    blocks = jax.vmap(one_source)(jax.random.split(source_key, DEVICES))
    blocks = blocks.reshape(N_SEQ, N_ROWS, TOK_DEV, LOOK).transpose(1, 0, 2, 3)
    return blocks.reshape(BATCH, LENGTH, LOOK).astype(jnp.int32)


def level_of(stream_key, extent, pieces, smallest, top_value):
    loudness, own = 1.0, jax.random.fold_in(stream_key, 6)
    for position, blocks in pieces:
        heights = jnp.exp(jax.random.uniform(jax.random.fold_in(own, position), (blocks,), jnp.float32, smallest / len(pieces), top_value / len(pieces)))
        loudness = loudness * jnp.repeat(heights, extent[position] // blocks).reshape([-1 if axis == position else 1 for axis in range(len(extent))])
    return loudness


def gaussian(own_key, shape, scale, reach, cuts=(), kind=jnp.bfloat16):
    entries = scale * jax.random.normal(own_key, shape, jnp.float32)
    if cuts:
        entries = entries * level_of(own_key, shape, cuts, -0.22, 0.18)
    return jnp.clip(entries, -reach, reach).astype(kind)


def setup_inputs(seed: int = 0) -> dict:
    key_list = jax.random.split(jax.random.key(seed), 11)
    hidden = gaussian(key_list[0], (BATCH, LENGTH, D), 1.0, 6.0, ((0, 16), (1, 8)))
    row_ids = draw_row_ids(jax.random.fold_in(key_list[10], 71), 0)
    table = gaussian(key_list[2], (TABLE_ROWS, RW), 1.0, 6.0, ((0, 128),))
    key_weight = gaussian(key_list[3], (MEM, D), MEM ** -0.5, 0.1875)
    value_weight = gaussian(key_list[4], (MEM, D), MEM ** -0.5, 0.1875)
    hidden_gain = jnp.clip(1.0 + 0.18 * jax.random.normal(key_list[5], (D,), jnp.float32), 0.1, 1.9)
    key_gain = jnp.clip(1.0 + 0.18 * jax.random.normal(key_list[6], (D,), jnp.float32), 0.1, 1.9)
    conv_gain = jnp.clip(1.0 + 0.18 * jax.random.normal(key_list[7], (D,), jnp.float32), 0.1, 1.9)
    conv_kernel = gaussian(key_list[8], (KW, D), 0.5, 3.0, (), jnp.float32)
    cotangent = gaussian(key_list[9], (BATCH, LENGTH, D), 1.0, 6.0, ((0, 16), (1, 8)))
    return dict(hidden=hidden, row_ids=row_ids, table=table, key_weight=key_weight, value_weight=value_weight, hidden_gain=hidden_gain, key_gain=key_gain, conv_gain=conv_gain, conv_kernel=conv_kernel, cotangent=cotangent)


EPSILON = 1e-06

def rms_apply(values, gain):
    scale = lax.rsqrt(lax.optimization_barrier(jnp.mean(values * values, axis=-1, keepdims=True)) + EPSILON)
    return (values * scale * gain, scale)

def rms_back(values, scale, gain, upstream):
    scaled = gain * upstream
    return scale * scaled - values * scale ** 3 * lax.optimization_barrier(jnp.mean(values * scaled, axis=-1, keepdims=True))

def reference(hidden, row_ids, table, key_weight, value_weight, hidden_gain, key_gain, conv_gain, conv_kernel, cotangent):
    root_width = jnp.sqrt(jnp.float32(D))

    def one_sequence(packed):
        hidden_seq, ids_seq, cot_seq = packed
        memory = table[ids_seq].reshape(LENGTH, MEM)
        key_proj = jnp.dot(memory, key_weight, preferred_element_type=jnp.float32)
        value_proj = jnp.dot(memory, value_weight, preferred_element_type=jnp.float32)
        states = hidden_seq.astype(jnp.float32)
        norm_hidden, hidden_scale = rms_apply(states, hidden_gain)
        norm_key, key_scale = rms_apply(key_proj, key_gain)
        gate_value = jax.nn.sigmoid(lax.optimization_barrier(jnp.sum(norm_hidden * norm_key, axis=-1, keepdims=True)) / root_width)
        gated_value = gate_value * value_proj
        conv_in, conv_scale = rms_apply(gated_value, conv_gain)
        padded = jnp.concatenate([jnp.zeros((KW - 1, D), jnp.float32), conv_in], axis=0)
        conv_out = jnp.zeros((LENGTH, D), jnp.float32)
        for offset in range(KW):
            conv_out = conv_out + conv_kernel[offset] * padded[KW - 1 - offset:KW - 1 - offset + LENGTH]
        conv_sigmoid = jax.nn.sigmoid(conv_out)
        mixed_out = (states + conv_out * conv_sigmoid + gated_value).astype(jnp.bfloat16)
        upstream = cot_seq.astype(jnp.float32)
        conv_grad = upstream * conv_sigmoid * (1.0 + conv_out * (1.0 - conv_sigmoid))
        padded_grad = jnp.concatenate([conv_grad, jnp.zeros((KW - 1, D), jnp.float32)], axis=0)
        in_grad = jnp.zeros((LENGTH, D), jnp.float32)
        for offset in range(KW):
            in_grad = in_grad + conv_kernel[offset] * padded_grad[offset:offset + LENGTH]
        gated_grad = upstream + rms_back(gated_value, conv_scale, conv_gain, in_grad)
        gate_grad = lax.optimization_barrier(jnp.sum(gated_grad * value_proj, axis=-1, keepdims=True))
        value_grad = gate_value * gated_grad
        score_grad = gate_grad * gate_value * (1.0 - gate_value) / root_width
        hidden_grad = upstream + rms_back(states, hidden_scale, hidden_gain, score_grad * norm_key)
        key_grad = rms_back(key_proj, key_scale, key_gain, score_grad * norm_hidden)
        memory_grad = jnp.dot(key_grad.astype(jnp.bfloat16), key_weight.T, preferred_element_type=jnp.float32)
        memory_grad = memory_grad + jnp.dot(value_grad.astype(jnp.bfloat16), value_weight.T, preferred_element_type=jnp.float32)
        return (mixed_out, hidden_grad.astype(jnp.bfloat16), memory_grad.reshape(LENGTH * LOOK, RW))
    mixed_all, hidden_all, memory_all = lax.map(one_sequence, (hidden, row_ids, cotangent))
    table_grad = jnp.zeros((TABLE_ROWS, RW), jnp.float32).at[row_ids.reshape(-1)].add(memory_all.reshape(-1, RW))
    return (mixed_all, hidden_all, table_grad)
```

```python
import functools
import math

import jax
import jax.numpy as jnp
from jax import lax
from jax.experimental import pallas as pl
from jax.experimental.pallas import tpu as pltpu
from jax.sharding import PartitionSpec as P

EPSILON = 1e-06
F32 = jnp.float32
BF16 = jnp.bfloat16
LANES = 128
NT = (((1,), (1,)), ((), ()))
VMEM = pl.BlockSpec(memory_space=pltpu.VMEM)
SMEM = pl.BlockSpec(memory_space=pltpu.SMEM)


def params(mib):
    return pltpu.CompilerParams(vmem_limit_bytes=mib << 20)


def shifted(block, axis, distance):
    devices = range(lax.axis_size(axis))
    route = [(i - distance, i) for i in devices if i - distance in devices]
    return lax.ppermute(block, axis, route)


def exchange(block):
    return lax.all_to_all(block, ("seq", "rows"), split_axis=0, concat_axis=0, tiled=True)


def route_kernel(rows_here, capacity, ids_ref, send_ref, slot_ref):
    lookups, tokens = ids_ref.shape
    owners = send_ref.shape[0]
    ids = ids_ref[...]
    shift = rows_here.bit_length() - 1
    owner_of = lax.shift_right_logical(ids, shift)
    code = (ids & (rows_here - 1)) + 1
    high = lax.shift_right_logical(code, 6).astype(F32)
    low = (code & 63).astype(F32)
    owner_axis = lax.broadcasted_iota(jnp.int32, (owners, tokens), 0)
    source = lax.broadcasted_iota(jnp.int32, (tokens, 2 * tokens), 0)
    target = lax.broadcasted_iota(jnp.int32, (tokens, 2 * tokens), 1)
    earlier = jnp.where(source < target, 1.0, 0.0).astype(BF16)
    ranks = 32
    rank_axis = lax.broadcasted_iota(jnp.int32, (ranks, tokens), 0)
    base = jnp.zeros((owners, tokens), F32)
    sent_high = jnp.zeros((owners, ranks), F32)
    sent_low = jnp.zeros((owners, ranks), F32)
    for look in range(lookups):
        owner_row = owner_of[look : look + 1, :]
        onehot = jnp.where(owner_axis == owner_row, 1.0, 0.0)
        packed = onehot.astype(BF16)
        counts = jnp.dot(packed, earlier, preferred_element_type=F32)
        before = counts[:, :tokens] + base
        base = base + counts[:, tokens:]
        rank = jnp.sum(onehot * before, axis=0, keepdims=True).astype(jnp.int32)
        slot_ref[look : look + 1, :] = owner_row * capacity + rank
        at_rank = rank_axis == rank
        high_at = jnp.where(at_rank, high[look : look + 1, :], 0.0).astype(BF16)
        low_at = jnp.where(at_rank, low[look : look + 1, :], 0.0).astype(BF16)
        sent_high += lax.dot_general(packed, high_at, NT, preferred_element_type=F32)
        sent_low += lax.dot_general(packed, low_at, NT, preferred_element_type=F32)
    send_ref[...] = jnp.zeros_like(send_ref)
    send_ref[:, :ranks] = (sent_high * 64.0 + sent_low).astype(jnp.int32)


def fetch_kernel(capacity, asked_ref, table_ref, found_ref, table_f32, found_f32):
    table_f32[...] = table_ref[...].astype(F32)

    def one_device(device, carry):
        first = pl.multiple_of(device * capacity, 8)
        for rank in range(capacity):
            row = jnp.maximum(asked_ref[device, rank] - 1, 0)
            found_f32[pl.ds(first + rank, 1), :] = table_f32[pl.ds(row, 1), :]
        return carry

    lax.fori_loop(0, asked_ref.shape[0], one_device, 0)
    found_ref[...] = found_f32[...].astype(BF16)


def forward_kernel(
    slot_ref, returned_ref, key_w_ref, value_w_ref, x_ref, c_ref, gain_ref,
    key_ref, value_ref, stat_ref, first_ref, last_ref,
    returned_f32, memory_f32, memory_ref,
):
    tokens, width = x_ref.shape
    lookups = slot_ref.shape[0]
    returned_f32[...] = returned_ref[...].astype(F32)
    unroll = 4

    def some_tokens(step, carry):
        for inner in range(unroll):
            token = step * unroll + inner
            for look in range(lookups):
                memory_f32[pl.ds(look * tokens + token, 1), :] = returned_f32[pl.ds(slot_ref[look, token], 1), :]
        return carry

    lax.fori_loop(0, tokens // unroll, some_tokens, 0)
    for look in range(lookups):
        memory_ref[:, look * LANES : (look + 1) * LANES] = memory_f32[look * tokens : (look + 1) * tokens, :].astype(BF16)
    memory = memory_ref[...]
    chunk = 512
    xx = kk = vv = xk = cv = jnp.zeros((tokens, LANES), F32)
    for start in range(0, width, chunk):
        key_ref[:, start : start + chunk] = jnp.dot(
            memory, key_w_ref[:, start : start + chunk], preferred_element_type=F32
        )
        value_ref[:, start : start + chunk] = jnp.dot(
            memory, value_w_ref[:, start : start + chunk], preferred_element_type=F32
        )
        for part in range(start, start + chunk, LANES):
            cols = slice(part, part + LANES)
            x = x_ref[:, cols].astype(F32)
            key = key_ref[:, cols]
            value = value_ref[:, cols]
            xx += x * x
            kk += key * key
            vv += value * value
            xk += x * key * gain_ref[:, cols]
            cv += c_ref[:, cols].astype(F32) * value
    xx, kk, vv, xk, cv = (jnp.sum(s, axis=-1, keepdims=True) for s in (xx, kk, vv, xk, cv))
    hidden_scale = lax.rsqrt(xx / width + EPSILON)
    key_scale = lax.rsqrt(kk / width + EPSILON)
    gate = jax.nn.sigmoid(hidden_scale * key_scale * xk / math.sqrt(width))
    conv_scale = lax.rsqrt(gate * gate * vv / width + EPSILON)
    for place, stat in enumerate((hidden_scale, key_scale, gate, conv_scale, xk, cv)):
        stat_ref[:, place : place + 1] = stat
    scaled = gate * conv_scale
    first_ref[...] = value_ref[:8, :] * scaled[:8]
    last_ref[...] = value_ref[tokens - 8 :, :] * scaled[tokens - 8 :]


def backward_kernel(
    slot_ref, key_ref, value_ref, stat_ref, x_ref, c_ref, gain_ref, taps_ref, earlier_ref, later_ref, later_c_ref,
    key_w_ref, value_w_ref,
    mixed_ref, coef_ref, grads_ref,
    conv_in, conv_grad, back, key_grad, value_grad, memory_grad, slots,
):
    tokens, width = x_ref.shape
    lookups = slot_ref.shape[0]
    taps = taps_ref.shape[0]
    hidden_scale, key_scale, gate, conv_scale, xk, cv = (stat_ref[:, i : i + 1] for i in range(6))
    wide = (tokens, LANES)
    gate_w = jnp.broadcast_to(gate, wide)
    scaled_w = jnp.broadcast_to(gate * conv_scale, wide)
    slots[...] = jnp.zeros_like(slots)
    uv = jnp.zeros(wide, F32)
    for start in range(0, width, LANES):
        cols = slice(start, start + LANES)
        value = value_ref[:, cols]
        conv_in[0:8, :] = earlier_ref[:, cols]
        conv_in[8 : 8 + tokens, :] = value * scaled_w
        conv_in[8 + tokens :, :] = later_ref[:, cols]
        conv_out = taps_ref[0:1, cols] * conv_in[8:, :]
        for tap in range(1, taps):
            conv_out += taps_ref[tap : tap + 1, cols] * conv_in[8 - tap : 16 + tokens - tap, :]
        sigmoid = jax.nn.sigmoid(conv_out)
        mixed_ref[:, cols] = (
            x_ref[:, cols].astype(F32) + (conv_out * sigmoid)[:tokens] + gate_w * value
        ).astype(BF16)
        slope = sigmoid * (1.0 + conv_out * (1.0 - sigmoid))
        conv_grad[0:tokens, :] = c_ref[:, cols].astype(F32) * slope[:tokens]
        conv_grad[tokens:, :] = later_c_ref[:, cols].astype(F32)[:8] * slope[tokens:]
        u = taps_ref[0:1, cols] * conv_grad[0:tokens, :]
        for tap in range(1, taps):
            u += taps_ref[tap : tap + 1, cols] * conv_grad[tap : tap + tokens, :]
        uv += u * value
        back[:, cols] = u
    uv = jnp.sum(uv, axis=-1, keepdims=True)
    cube = conv_scale * conv_scale * conv_scale
    gate_grad = cv + EPSILON * cube * uv
    score_grad = gate_grad * gate * (1.0 - gate) / math.sqrt(width)
    both = score_grad * hidden_scale * key_scale
    from_hidden = both * hidden_scale * hidden_scale * xk / width
    from_key = both * key_scale * key_scale * xk / width
    from_value = gate * gate * cube * uv / width
    coef_ref[:, 0:1] = both
    coef_ref[:, 1:2] = from_hidden
    both_w = jnp.broadcast_to(both, wide)
    key_w = jnp.broadcast_to(from_key, wide)
    value_w = jnp.broadcast_to(gate * from_value, wide)
    scaled_w = jnp.broadcast_to(gate * conv_scale, wide)
    gate_w = jnp.broadcast_to(gate, wide)
    for start in range(0, width, LANES):
        cols = slice(start, start + LANES)
        value_grad[:, cols] = (
            gate_w * c_ref[:, cols].astype(F32) + scaled_w * back[:, cols] - value_w * value_ref[:, cols]
        ).astype(BF16)
        key_grad[:, cols] = (
            both_w * gain_ref[:, cols] * x_ref[:, cols].astype(F32) - key_w * key_ref[:, cols]
        ).astype(BF16)
    span = 256
    for start in range(0, lookups * LANES, span):
        rows = slice(start, start + span)
        both_looks = lax.dot_general(
            key_grad[...], key_w_ref[rows, :], NT, preferred_element_type=F32
        ) + lax.dot_general(value_grad[...], value_w_ref[rows, :], NT, preferred_element_type=F32)
        for part in range(0, span, LANES):
            look = (start + part) // LANES
            memory_grad[look * tokens : (look + 1) * tokens, :] = both_looks[:, part : part + LANES]
    unroll = 4

    def some_tokens(step, carry):
        for inner in range(unroll):
            token = step * unroll + inner
            for look in range(lookups):
                slots[pl.ds(slot_ref[look, token], 1), :] = memory_grad[pl.ds(look * tokens + token, 1), :]
        return carry

    lax.fori_loop(0, tokens // unroll, some_tokens, 0)
    grads_ref[...] = slots[...].astype(BF16)


def hidden_kernel(key_ref, coef_ref, x_ref, c_ref, gain_ref, out_ref):
    tokens, width = x_ref.shape
    both = jnp.broadcast_to(coef_ref[:, 0:1], (tokens, LANES))
    own = jnp.broadcast_to(coef_ref[:, 1:2], (tokens, LANES))
    for start in range(0, width, LANES):
        cols = slice(start, start + LANES)
        out_ref[:, cols] = (
            c_ref[:, cols].astype(F32)
            + both * gain_ref[:, cols] * key_ref[:, cols]
            - own * x_ref[:, cols].astype(F32)
        ).astype(BF16)


def add_kernel(capacity, asked_ref, arrived_ref, out_ref, arrived, *others):
    totals = (out_ref, *others)
    ways = len(totals)
    for total in totals:
        total[...] = jnp.zeros_like(total)
    arrived[...] = arrived_ref[...].astype(F32)

    def one_device(device, carry):
        first = pl.multiple_of(device * capacity, 8)
        for group in range(0, capacity, ways):
            rows = [jnp.maximum(asked_ref[device, group + way] - 1, 0) for way in range(ways)]
            sums = [
                totals[way][pl.ds(rows[way], 1), :] + arrived[pl.ds(first + group + way, 1), :]
                for way in range(ways)
            ]
            for way in range(ways):
                totals[way][pl.ds(rows[way], 1), :] = sums[way]
        return carry

    lax.fori_loop(0, asked_ref.shape[0], one_device, 0)
    total = out_ref[...]
    for other in others:
        total = total + other[...]
    out_ref[...] = total


def shards(
    hidden, row_ids, table, key_weight, value_weight, hidden_gain, key_gain, conv_gain, conv_kernel, cotangent
):
    tokens, width = hidden.shape[1:]
    lookups = row_ids.shape[2]
    rows_here, row_width = table.shape
    devices = lax.axis_size(("seq", "rows"))
    capacity = 3 * tokens * lookups // devices
    places = devices * capacity
    x, c = hidden[0], cotangent[0]
    gain = (hidden_gain * key_gain)[None]
    taps = conv_kernel * conv_gain[None]
    shape = jax.ShapeDtypeStruct

    send, slot_of = pl.pallas_call(
        functools.partial(route_kernel, rows_here, capacity),
        out_shape=(shape((devices, LANES), jnp.int32), shape((lookups, tokens), jnp.int32)),
        in_specs=[VMEM],
        out_specs=(VMEM, VMEM),
        name="route",
    )(row_ids[0].T)
    asked = exchange(send)
    found = pl.pallas_call(
        functools.partial(fetch_kernel, capacity),
        out_shape=shape((places, row_width), BF16),
        in_specs=[SMEM, VMEM],
        out_specs=VMEM,
        scratch_shapes=[pltpu.VMEM((rows_here, row_width), F32), pltpu.VMEM((places, row_width), F32)],
        compiler_params=params(12),
        name="fetch",
    )(asked, table)
    returned = exchange(found.reshape(devices, capacity, row_width)).reshape(places, row_width)
    later_c = shifted(c[:16], "seq", -1)
    key, value, stats, first, last = pl.pallas_call(
        forward_kernel,
        out_shape=(
            shape((tokens, width), F32),
            shape((tokens, width), F32),
            shape((tokens, LANES), F32),
            shape((8, width), F32),
            shape((8, width), F32),
        ),
        in_specs=[SMEM] + [VMEM] * 6,
        out_specs=(VMEM,) * 5,
        scratch_shapes=[
            pltpu.VMEM((places, row_width), F32),
            pltpu.VMEM((tokens * lookups, row_width), F32),
            pltpu.VMEM((tokens, lookups * row_width), BF16),
        ],
        compiler_params=params(12),
        name="forward",
    )(slot_of, returned, key_weight, value_weight, x, c, gain)
    earlier = shifted(last, "seq", 1)
    later = shifted(first, "seq", -1)
    mixed, coef, grads = pl.pallas_call(
        backward_kernel,
        out_shape=(shape((tokens, width), BF16), shape((tokens, LANES), F32), shape((places, row_width), BF16)),
        in_specs=[SMEM] + [VMEM] * 12,
        out_specs=(VMEM,) * 3,
        scratch_shapes=[
            pltpu.VMEM((tokens + 16, LANES), F32),
            pltpu.VMEM((tokens + 8, LANES), F32),
            pltpu.VMEM((tokens, width), F32),
            pltpu.VMEM((tokens, width), BF16),
            pltpu.VMEM((tokens, width), BF16),
            pltpu.VMEM((tokens * lookups, row_width), F32),
            pltpu.VMEM((places, row_width), F32),
        ],
        compiler_params=params(16),
        name="backward",
    )(slot_of, key, value, stats, x, c, gain, taps, earlier, later, later_c, key_weight, value_weight)
    arrived = exchange(grads.reshape(devices, capacity, row_width)).reshape(places, row_width)
    hidden_grad = pl.pallas_call(
        hidden_kernel,
        out_shape=shape((tokens, width), BF16),
        in_specs=[VMEM] * 5,
        out_specs=VMEM,
        cost_estimate=pl.CostEstimate(flops=5 * tokens * width, bytes_accessed=10 * tokens * width, transcendentals=0),
        name="hidden",
    )(key, coef, x, c, gain)
    ways = 8
    table_grad = pl.pallas_call(
        functools.partial(add_kernel, capacity),
        out_shape=shape((rows_here, row_width), F32),
        in_specs=[SMEM, VMEM],
        out_specs=VMEM,
        scratch_shapes=[pltpu.VMEM((places, row_width), F32)]
        + [pltpu.VMEM((rows_here, row_width), F32)] * (ways - 1),
        compiler_params=params(24),
        name="add",
    )(asked, arrived)
    return (mixed[None], hidden_grad[None], table_grad)


def solution(mesh):
    seq_block = P("rows", "seq", None)
    table_block = P(("seq", "rows"), None)
    return jax.shard_map(
        shards,
        mesh=mesh,
        in_specs=(seq_block, seq_block, table_block, P(), P(), P(), P(), P(), P(), seq_block),
        out_specs=(seq_block, seq_block, table_block),
        check_vma=False,
    )
```

```python
import functools
import math

import jax
import jax.numpy as jnp
from jax import lax
from jax.experimental import pallas as pl
from jax.experimental.pallas import tpu as pltpu
from jax.sharding import PartitionSpec as P

EPSILON = 1e-06
F32 = jnp.float32
BF16 = jnp.bfloat16
LANES = 128
NT = (((1,), (1,)), ((), ()))
VMEM = pl.BlockSpec(memory_space=pltpu.VMEM)
SMEM = pl.BlockSpec(memory_space=pltpu.SMEM)
ANY = pl.BlockSpec(memory_space=pl.ANY)


def params(mib):
    return pltpu.CompilerParams(vmem_limit_bytes=mib << 20)


def in_hbm(x):
    return pltpu.with_memory_space_constraint(x, pltpu.HBM)


def in_vmem(x):
    return pltpu.with_memory_space_constraint(x, pltpu.VMEM)


def shifted(block, axis, distance):
    devices = lax.axis_size(axis)
    return lax.ppermute(block, axis, [(i, (i + distance) % devices) for i in range(devices)])


def exchange(block):
    return lax.all_to_all(block, ("seq", "rows"), split_axis=0, concat_axis=0, tiled=True)


def route_kernel(rows_here, capacity, ids_ref, send_ref, slot_ref):
    lookups, tokens = ids_ref.shape
    owners = send_ref.shape[0]
    ids = ids_ref[...]
    shift = rows_here.bit_length() - 1
    owner_of = lax.shift_right_logical(ids, shift)
    code = (ids & (rows_here - 1)) + 1
    high = lax.shift_right_logical(code, 6).astype(F32)
    low = (code & 63).astype(F32)
    owner_axis = lax.broadcasted_iota(jnp.int32, (owners, tokens), 0)
    source = lax.broadcasted_iota(jnp.int32, (tokens, 2 * tokens), 0)
    target = lax.broadcasted_iota(jnp.int32, (tokens, 2 * tokens), 1)
    earlier = jnp.where(source < target, 1.0, 0.0).astype(BF16)
    ranks = 32
    rank_axis = lax.broadcasted_iota(jnp.int32, (ranks, tokens), 0)
    base = jnp.zeros((owners, tokens), F32)
    sent_high = jnp.zeros((owners, ranks), F32)
    sent_low = jnp.zeros((owners, ranks), F32)
    for look in range(lookups):
        owner_row = owner_of[look : look + 1, :]
        onehot = jnp.where(owner_axis == owner_row, 1.0, 0.0)
        packed = onehot.astype(BF16)
        counts = jnp.dot(packed, earlier, preferred_element_type=F32)
        before = counts[:, :tokens] + base
        base = base + counts[:, tokens:]
        rank = jnp.sum(onehot * before, axis=0, keepdims=True).astype(jnp.int32)
        slot_ref[look : look + 1, :] = owner_row * capacity + rank
        at_rank = rank_axis == rank
        high_at = jnp.where(at_rank, high[look : look + 1, :], 0.0).astype(BF16)
        low_at = jnp.where(at_rank, low[look : look + 1, :], 0.0).astype(BF16)
        sent_high += lax.dot_general(packed, high_at, NT, preferred_element_type=F32)
        sent_low += lax.dot_general(packed, low_at, NT, preferred_element_type=F32)
    send_ref[...] = jnp.zeros_like(send_ref)
    send_ref[:, :ranks] = (sent_high * 64.0 + sent_low).astype(jnp.int32)


def stage_table_kernel(after_ref, table_hbm, out_ref, arrived):
    del after_ref
    copy = pltpu.make_async_copy(table_hbm, out_ref, arrived)
    copy.start()
    copy.wait()


def fetch_kernel(capacity, asked_ref, table_ref, found_hbm, asked_t_ref, asked_smem, table_f32, found_f32, found, turned, left):
    devices = asked_ref.shape[0]
    asked_t_ref[...] = jnp.maximum(asked_ref[...].T[:capacity, :] - 1, 0)
    to_smem = pltpu.make_async_copy(asked_t_ref, asked_smem, turned)
    to_smem.start()
    table_f32[...] = table_ref[...].astype(F32)
    to_smem.wait()
    pieces = left.shape[0]
    each = devices // pieces
    copies = []
    for piece in range(pieces):

        def one_rank(rank, carry, first=piece * each):
            for device in range(first, first + each):
                found_f32[pl.ds(rank + device * capacity, 1), :] = table_f32[pl.ds(asked_smem[rank, device], 1), :]
            return carry

        lax.fori_loop(0, capacity, one_rank, 0)
        part = pl.ds(piece * each * capacity, each * capacity)
        found[part, :] = found_f32[part, :].astype(BF16)
        copies.append(pltpu.make_async_copy(found.at[part], found_hbm.at[part], left.at[piece]))
        copies[-1].start()
    for copy in copies:
        copy.wait()


def forward_kernel(
    slot_ref, returned_ref, key_w_hbm, value_w_hbm, x_ref, c_ref, gain_ref,
    key_ref, value_ref, stat_ref, first_ref, last_ref,
    returned_f32, memory_f32, memory_ref, key_w_ref, value_w_ref, came,
):
    tokens, width = x_ref.shape
    chunk = 512
    weights = []
    for place in range(width // chunk):
        columns = pl.ds(place * chunk, chunk)
        for which, (source, weight) in enumerate(((key_w_hbm, key_w_ref), (value_w_hbm, value_w_ref))):
            weights.append(
                pltpu.make_async_copy(source.at[:, columns], weight.at[:, columns], came.at[2 * place + which])
            )
            weights[-1].start()
    lookups = slot_ref.shape[0]
    returned_f32[...] = returned_ref[...].astype(F32)
    unroll = 4

    def some_tokens(step, carry):
        for inner in range(unroll):
            token = step * unroll + inner
            for look in range(lookups):
                memory_f32[pl.ds(look * tokens + token, 1), :] = returned_f32[pl.ds(slot_ref[look, token], 1), :]
        return carry

    lax.fori_loop(0, tokens // unroll, some_tokens, 0)
    for look in range(lookups):
        memory_ref[:, look * LANES : (look + 1) * LANES] = memory_f32[look * tokens : (look + 1) * tokens, :].astype(BF16)
    memory = memory_ref[...]
    xx = kk = vv = xk = cv = jnp.zeros((tokens, LANES), F32)
    for start in range(0, width, chunk):
        weights[start // chunk * 2].wait()
        weights[start // chunk * 2 + 1].wait()
        key_ref[:, start : start + chunk] = jnp.dot(
            memory, key_w_ref[:, start : start + chunk], preferred_element_type=F32
        )
        value_ref[:, start : start + chunk] = jnp.dot(
            memory, value_w_ref[:, start : start + chunk], preferred_element_type=F32
        )
        for part in range(start, start + chunk, LANES):
            cols = slice(part, part + LANES)
            x = x_ref[:, cols].astype(F32)
            key = key_ref[:, cols]
            value = value_ref[:, cols]
            xx += x * x
            kk += key * key
            vv += value * value
            xk += x * key * gain_ref[:, cols]
            cv += c_ref[:, cols].astype(F32) * value
    xx, kk, vv, xk, cv = (jnp.sum(s, axis=-1, keepdims=True) for s in (xx, kk, vv, xk, cv))
    hidden_scale = lax.rsqrt(xx / width + EPSILON)
    key_scale = lax.rsqrt(kk / width + EPSILON)
    gate = jax.nn.sigmoid(hidden_scale * key_scale * xk / math.sqrt(width))
    conv_scale = lax.rsqrt(gate * gate * vv / width + EPSILON)
    for place, stat in enumerate((hidden_scale, key_scale, gate, conv_scale, xk, cv)):
        stat_ref[:, place : place + 1] = stat
    scaled = gate * conv_scale
    first_ref[...] = value_ref[:8, :] * scaled[:8]
    last_ref[...] = value_ref[tokens - 8 :, :] * scaled[tokens - 8 :]


def slope_of(conv_out):
    sigmoid = jax.nn.sigmoid(conv_out)
    return sigmoid * (1.0 + conv_out * (1.0 - sigmoid))


def alone_kernel(
    value_ref, stat_ref, c_ref, taps_ref, key_w_hbm, value_w_hbm,
    conv_ref, back_ref, uv_ref, key_w_ref, value_w_ref,
    conv_in, conv_grad, came,
):
    weights = [
        pltpu.make_async_copy(key_w_hbm, key_w_ref, came.at[0]),
        pltpu.make_async_copy(value_w_hbm, value_w_ref, came.at[1]),
    ]
    for weight in weights:
        weight.start()
    tokens, width = value_ref.shape
    taps = taps_ref.shape[0]
    wide = (tokens, LANES)
    scaled = jnp.broadcast_to(stat_ref[:, 2:3] * stat_ref[:, 3:4], wide)
    conv_in[0:8, :] = jnp.zeros((8, LANES), F32)
    conv_grad[tokens:, :] = jnp.zeros((8, LANES), F32)
    uv_ref[...] = jnp.zeros(wide, F32)
    for start in range(0, width, LANES):
        cols = slice(start, start + LANES)
        conv_in[8:, :] = value_ref[:, cols] * scaled
        conv_out = taps_ref[0:1, cols] * conv_in[8:, :]
        for tap in range(1, taps):
            conv_out += taps_ref[tap : tap + 1, cols] * conv_in[8 - tap : 8 + tokens - tap, :]
        conv_ref[:, cols] = conv_out
        conv_grad[0:tokens, :] = c_ref[:, cols].astype(F32) * slope_of(conv_out)
        u = taps_ref[0:1, cols] * conv_grad[0:tokens, :]
        for tap in range(1, taps):
            u += taps_ref[tap : tap + 1, cols] * conv_grad[tap : tap + tokens, :]
        back_ref[:, cols] = u
        uv_ref[...] += u * value_ref[:, cols]
    for weight in weights:
        weight.wait()


def finish_kernel(
    slot_ref, key_ref, value_ref, stat_ref, x_ref, c_ref, gain_ref, taps_ref, conv_ref, back_ref, uv_ref,
    earlier_ref, later_ref, later_c_ref, key_w_ref, value_w_ref,
    coef_hbm, head_hbm, grads_hbm,
    coef_ref, head_ref, sent, rim, rim_grad, rim_back, rim_uv, key_grad, value_grad, memory_grad, slots, packed, left,
):
    tokens, width = x_ref.shape
    lookups = slot_ref.shape[0]
    taps = taps_ref.shape[0]
    seq = lax.axis_index("seq")
    has_earlier = jnp.where(seq > 0, 1.0, 0.0)
    has_later = jnp.where(seq < lax.axis_size("seq") - 1, 1.0, 0.0)
    hidden_scale, key_scale, gate, conv_scale, xk, cv = (stat_ref[:, i : i + 1] for i in range(6))
    scaled = gate * conv_scale
    last = slice(tokens - 8, tokens)
    rim_uv[...] = jnp.zeros_like(rim_uv)
    rim[8:16, :] = jnp.zeros((8, LANES), F32)
    rim_grad[0:8, :] = jnp.zeros((8, LANES), F32)
    rim_grad[16:24, :] = jnp.zeros((8, LANES), F32)
    slots[...] = jnp.zeros_like(slots)
    for start in range(0, width, LANES):
        cols = slice(start, start + LANES)
        weights = [taps_ref[tap : tap + 1, cols] for tap in range(taps)]
        alone = conv_ref[0:8, cols]
        rim[0:8, :] = earlier_ref[:, cols] * has_earlier
        joined = alone
        for tap in range(1, taps):
            joined += weights[tap] * rim[8 - tap : 16 - tap, :]
        head_ref[:, cols] = joined
        rim_grad[8:16, :] = c_ref[0:16, cols].astype(F32)[:8] * (slope_of(joined) - slope_of(alone))
        u = back_ref[0:8, cols]
        for tap in range(taps):
            u += weights[tap] * rim_grad[8 + tap : 16 + tap, :]
        rim_back[0:8, cols] = u
        rim_uv[0:8, :] += u * value_ref[0:8, cols]
        rim[16:24, :] = value_ref[last, cols] * scaled[last]
        rim[24:32, :] = later_ref[:, cols] * has_later
        beyond = weights[0] * rim[24:32, :]
        for tap in range(1, taps):
            beyond += weights[tap] * rim[24 - tap : 32 - tap, :]
        rim_grad[32:40, :] = later_c_ref[:, cols].astype(F32)[:8] * slope_of(beyond) * has_later
        u = back_ref[last, cols]
        rim_grad[24:32, :] = jnp.zeros((8, LANES), F32)
        for tap in range(1, taps):
            u += weights[tap] * rim_grad[24 + tap : 32 + tap, :]
        rim_back[8:16, cols] = u
        rim_uv[8:16, :] += u * value_ref[last, cols]
    uv = jnp.sum(
        jnp.concatenate([rim_uv[0:8, :], uv_ref[8 : tokens - 8, :], rim_uv[8:16, :]], axis=0), axis=-1, keepdims=True
    )
    cube = conv_scale * conv_scale * conv_scale
    gate_grad = cv + EPSILON * cube * uv
    score_grad = gate_grad * gate * (1.0 - gate) / math.sqrt(width)
    both = score_grad * hidden_scale * key_scale
    from_hidden = both * hidden_scale * hidden_scale * xk / width
    from_key = both * key_scale * key_scale * xk / width
    from_value = gate * gate * cube * uv / width
    coef_ref[:, 0:1] = both
    coef_ref[:, 1:2] = from_hidden
    coef_ref[:, 2:3] = gate
    small = [
        pltpu.make_async_copy(coef_ref, coef_hbm, sent.at[0]),
        pltpu.make_async_copy(head_ref, head_hbm, sent.at[1]),
    ]
    for copy in small:
        copy.start()
    wide = (tokens, LANES)
    both_w = jnp.broadcast_to(both, wide)
    key_w = jnp.broadcast_to(from_key, wide)
    value_w = jnp.broadcast_to(gate * from_value, wide)
    scaled_w = jnp.broadcast_to(scaled, wide)
    gate_w = jnp.broadcast_to(gate, wide)
    for start in range(0, width, LANES):
        cols = slice(start, start + LANES)
        u = jnp.concatenate([rim_back[0:8, cols], back_ref[8 : tokens - 8, cols], rim_back[8:16, cols]], axis=0)
        value_grad[:, cols] = (
            gate_w * c_ref[:, cols].astype(F32) + scaled_w * u - value_w * value_ref[:, cols]
        ).astype(BF16)
        key_grad[:, cols] = (
            both_w * gain_ref[:, cols] * x_ref[:, cols].astype(F32) - key_w * key_ref[:, cols]
        ).astype(BF16)
    span = 256
    for start in range(0, lookups * LANES, span):
        rows = slice(start, start + span)
        both_looks = lax.dot_general(
            key_grad[...], key_w_ref[rows, :], NT, preferred_element_type=F32
        ) + lax.dot_general(value_grad[...], value_w_ref[rows, :], NT, preferred_element_type=F32)
        for part in range(0, span, LANES):
            look = (start + part) // LANES
            memory_grad[look * tokens : (look + 1) * tokens, :] = both_looks[:, part : part + LANES]
    unroll = 4

    def some_tokens(step, carry):
        for inner in range(unroll):
            token = step * unroll + inner
            for look in range(lookups):
                slots[pl.ds(slot_ref[look, token], 1), :] = memory_grad[pl.ds(look * tokens + token, 1), :]
        return carry

    lax.fori_loop(0, tokens // unroll, some_tokens, 0)
    pieces = left.shape[0]
    rows = slots.shape[0] // pieces
    copies = []
    for piece in range(pieces):
        part = pl.ds(piece * rows, rows)
        packed[part, :] = slots[part, :].astype(BF16)
        copies.append(pltpu.make_async_copy(packed.at[part], grads_hbm.at[part], left.at[piece]))
        copies[-1].start()
    for copy in small + copies:
        copy.wait()


def outputs_kernel(key_ref, value_ref, coef_ref, x_ref, c_ref, gain_ref, conv_ref, head_ref, mixed_ref, hidden_ref):
    tokens, width = x_ref.shape
    both, own, gate = (jnp.broadcast_to(coef_ref[:, i : i + 1], (tokens, LANES)) for i in range(3))
    for start in range(0, width, LANES):
        cols = slice(start, start + LANES)
        x = x_ref[:, cols].astype(F32)
        conv_out = jnp.concatenate([head_ref[:, cols], conv_ref[8:, cols]], axis=0)
        mixed_ref[:, cols] = (x + conv_out * jax.nn.sigmoid(conv_out) + gate * value_ref[:, cols]).astype(BF16)
        hidden_ref[:, cols] = (
            c_ref[:, cols].astype(F32) + both * gain_ref[:, cols] * key_ref[:, cols] - own * x
        ).astype(BF16)


def add_kernel(asked_ref, arrived_ref, out_ref, asked_smem, moved, arrived, *others):
    to_smem = pltpu.make_async_copy(asked_ref, asked_smem, moved)
    to_smem.start()
    totals = (out_ref, *others)
    ways = len(totals)
    capacity, devices = asked_ref.shape
    for total in totals:
        total[...] = jnp.zeros_like(total)
    arrived[...] = arrived_ref[...].astype(F32)
    to_smem.wait()

    def one_rank(rank, carry):
        for group in range(0, devices, ways):
            rows = [asked_smem[rank, group + way] for way in range(ways)]
            sums = [
                totals[way][pl.ds(rows[way], 1), :] + arrived[pl.ds(rank + (group + way) * capacity, 1), :]
                for way in range(ways)
            ]
            for way in range(ways):
                totals[way][pl.ds(rows[way], 1), :] = sums[way]
        return carry

    lax.fori_loop(0, capacity, one_rank, 0)
    total = out_ref[...]
    for other in others:
        total = total + other[...]
    out_ref[...] = total


def shards(
    hidden, row_ids, table, key_weight, value_weight, hidden_gain, key_gain, conv_gain, conv_kernel, cotangent
):
    tokens, width = hidden.shape[1:]
    lookups = row_ids.shape[2]
    rows_here, row_width = table.shape
    devices = lax.axis_size(("seq", "rows"))
    capacity = 3 * tokens * lookups // devices
    places = devices * capacity
    x, c = hidden[0], cotangent[0]
    gain = (hidden_gain * key_gain)[None]
    taps = conv_kernel * conv_gain[None]
    shape = jax.ShapeDtypeStruct

    send, slot_of = pl.pallas_call(
        functools.partial(route_kernel, rows_here, capacity),
        out_shape=(shape((devices, LANES), jnp.int32), shape((lookups, tokens), jnp.int32)),
        in_specs=[VMEM],
        out_specs=(VMEM, VMEM),
        name="route",
    )(row_ids[0].T)
    asked = exchange(send)
    table_here = pl.pallas_call(
        stage_table_kernel,
        out_shape=shape((rows_here, row_width), BF16),
        in_specs=[VMEM, ANY],
        out_specs=VMEM,
        scratch_shapes=[pltpu.SemaphoreType.DMA],
        compiler_params=params(4),
        cost_estimate=pl.CostEstimate(flops=places * row_width, bytes_accessed=6 * places * row_width, transcendentals=0),
        name="stage_table",
    )(slot_of, in_hbm(table))
    found, asked_t = pl.pallas_call(
        functools.partial(fetch_kernel, capacity),
        out_shape=(pltpu.HBM((places, row_width), BF16), shape((capacity, devices), jnp.int32)),
        in_specs=[VMEM, VMEM],
        out_specs=(ANY, VMEM),
        scratch_shapes=[
            pltpu.SMEM((capacity, devices), jnp.int32),
            pltpu.VMEM((rows_here, row_width), F32),
            pltpu.VMEM((places, row_width), F32),
            pltpu.VMEM((places, row_width), BF16),
            pltpu.SemaphoreType.DMA,
            pltpu.SemaphoreType.DMA((4,)),
        ],
        compiler_params=params(8),
        name="fetch",
    )(asked, table_here)
    returned = exchange(found.reshape(devices, capacity, row_width)).reshape(places, row_width)
    later_c = shifted(c[:16], "seq", -1)
    key, value, stats, first, last = pl.pallas_call(
        forward_kernel,
        out_shape=(
            shape((tokens, width), F32),
            shape((tokens, width), F32),
            shape((tokens, LANES), F32),
            shape((8, width), F32),
            shape((8, width), F32),
        ),
        in_specs=[SMEM, VMEM, ANY, ANY, VMEM, VMEM, VMEM],
        out_specs=(VMEM,) * 5,
        scratch_shapes=[
            pltpu.VMEM((places, row_width), F32),
            pltpu.VMEM((tokens * lookups, row_width), F32),
            pltpu.VMEM((tokens, lookups * row_width), BF16),
            pltpu.VMEM(key_weight.shape, BF16),
            pltpu.VMEM(value_weight.shape, BF16),
            pltpu.SemaphoreType.DMA((width // 256,)),
        ],
        compiler_params=params(20),
        name="forward",
    )(slot_of, returned, in_hbm(key_weight), in_hbm(value_weight), x, c, gain)
    earlier = shifted(last, "seq", 1)
    later = shifted(first, "seq", -1)
    conv_out, back, uv, key_w, value_w = pl.pallas_call(
        alone_kernel,
        out_shape=(
            shape((tokens, width), F32),
            shape((tokens, width), F32),
            shape((tokens, LANES), F32),
            shape(key_weight.shape, BF16),
            shape(value_weight.shape, BF16),
        ),
        in_specs=[VMEM] * 4 + [ANY] * 2,
        out_specs=(VMEM,) * 5,
        scratch_shapes=[
            pltpu.VMEM((tokens + 8, LANES), F32),
            pltpu.VMEM((tokens + 8, LANES), F32),
            pltpu.SemaphoreType.DMA((2,)),
        ],
        compiler_params=params(4),
        cost_estimate=pl.CostEstimate(
            flops=40 * tokens * width, bytes_accessed=4 * key_weight.size, transcendentals=2 * tokens * width
        ),
        name="alone",
    )(value, stats, c, taps, in_hbm(key_weight), in_hbm(value_weight))
    coef, head, grads = pl.pallas_call(
        finish_kernel,
        out_shape=(
            pltpu.HBM((tokens, LANES), F32),
            pltpu.HBM((8, width), F32),
            pltpu.HBM((places, row_width), BF16),
        ),
        in_specs=[SMEM] + [VMEM] * 15,
        out_specs=(ANY,) * 3,
        scratch_shapes=[
            pltpu.VMEM((tokens, LANES), F32),
            pltpu.VMEM((8, width), F32),
            pltpu.SemaphoreType.DMA((2,)),
            pltpu.VMEM((32, LANES), F32),
            pltpu.VMEM((40, LANES), F32),
            pltpu.VMEM((16, width), F32),
            pltpu.VMEM((16, LANES), F32),
            pltpu.VMEM((tokens, width), BF16),
            pltpu.VMEM((tokens, width), BF16),
            pltpu.VMEM((tokens * lookups, row_width), F32),
            pltpu.VMEM((places, row_width), F32),
            pltpu.VMEM((places, row_width), BF16),
            pltpu.SemaphoreType.DMA((4,)),
        ],
        compiler_params=params(12),
        name="finish",
    )(slot_of, key, value, stats, x, c, gain, taps, conv_out, back, uv, earlier, later, later_c, key_w, value_w)
    arrived = exchange(grads.reshape(devices, capacity, row_width)).reshape(places, row_width)
    mixed, hidden_grad = pl.pallas_call(
        outputs_kernel,
        out_shape=(shape((tokens, width), BF16), shape((tokens, width), BF16)),
        in_specs=[VMEM] * 8,
        out_specs=(VMEM, VMEM),
        cost_estimate=pl.CostEstimate(
            flops=10 * tokens * width, bytes_accessed=20 * tokens * width, transcendentals=tokens * width
        ),
        name="outputs",
    )(key, value, coef, x, c, gain, conv_out, head)
    ways = 8
    table_grad = pl.pallas_call(
        add_kernel,
        out_shape=shape((rows_here, row_width), F32),
        in_specs=[VMEM, VMEM],
        out_specs=VMEM,
        scratch_shapes=[
            pltpu.SMEM((capacity, devices), jnp.int32),
            pltpu.SemaphoreType.DMA,
            pltpu.VMEM((places, row_width), F32),
        ]
        + [pltpu.VMEM((rows_here, row_width), F32)] * (ways - 1),
        compiler_params=params(24),
        name="add",
    )(asked_t, arrived)
    return (mixed[None], hidden_grad[None], table_grad)


def solution(mesh):
    seq_block = P("rows", "seq", None)
    table_block = P(("seq", "rows"), None)
    return jax.shard_map(
        shards,
        mesh=mesh,
        in_specs=(seq_block, seq_block, table_block, P(), P(), P(), P(), P(), P(), seq_block),
        out_specs=(seq_block, seq_block, table_block),
        check_vma=False,
    )
```

```python
import functools
import math

import jax
import jax.numpy as jnp
from jax import lax
from jax.experimental import pallas as pl
from jax.experimental.pallas import tpu as pltpu
from jax.sharding import PartitionSpec as P

EPSILON = 1e-06
F32 = jnp.float32
BF16 = jnp.bfloat16
LANES = 128
NT = (((1,), (1,)), ((), ()))
VMEM = pl.BlockSpec(memory_space=pltpu.VMEM)
SMEM = pl.BlockSpec(memory_space=pltpu.SMEM)
ANY = pl.BlockSpec(memory_space=pl.ANY)


def params(mib):
    return pltpu.CompilerParams(vmem_limit_bytes=mib << 20)


def in_hbm(x):
    return pltpu.with_memory_space_constraint(x, pltpu.HBM)


def in_vmem(x):
    return pltpu.with_memory_space_constraint(x, pltpu.VMEM)


def shifted(block, axis, distance):
    devices = lax.axis_size(axis)
    return lax.ppermute(block, axis, [(i, (i + distance) % devices) for i in range(devices)])


def exchange(block):
    return lax.all_to_all(block, ("seq", "rows"), split_axis=0, concat_axis=0, tiled=True)


def route_kernel(rows_here, capacity, ids_ref, send_ref, slot_ref):
    lookups, tokens = ids_ref.shape
    owners = send_ref.shape[0]
    ids = ids_ref[...]
    shift = rows_here.bit_length() - 1
    owner_of = lax.shift_right_logical(ids, shift)
    code = (ids & (rows_here - 1)) + 1
    high = lax.shift_right_logical(code, 6).astype(F32)
    low = (code & 63).astype(F32)
    owner_axis = lax.broadcasted_iota(jnp.int32, (owners, tokens), 0)
    source = lax.broadcasted_iota(jnp.int32, (tokens, 2 * tokens), 0)
    target = lax.broadcasted_iota(jnp.int32, (tokens, 2 * tokens), 1)
    earlier = jnp.where(source < target, 1.0, 0.0).astype(BF16)
    ranks = 32
    rank_axis = lax.broadcasted_iota(jnp.int32, (ranks, tokens), 0)
    onehots = [jnp.where(owner_axis == owner_of[look : look + 1, :], 1.0, 0.0) for look in range(lookups)]
    counts = jnp.dot(jnp.concatenate(onehots, axis=0).astype(BF16), earlier, preferred_element_type=F32)
    base = jnp.zeros((owners, tokens), F32)
    high_at, low_at = [], []
    for look in range(lookups):
        here = counts[look * owners : (look + 1) * owners]
        rank = jnp.sum(onehots[look] * (here[:, :tokens] + base), axis=0, keepdims=True).astype(jnp.int32)
        base = base + here[:, tokens:]
        slot_ref[look : look + 1, :] = owner_of[look : look + 1, :] * capacity + rank
        at_rank = rank_axis == rank
        high_at.append(jnp.where(at_rank, high[look : look + 1, :], 0.0))
        low_at.append(jnp.where(at_rank, low[look : look + 1, :], 0.0))
    onehot = jnp.concatenate(onehots, axis=1).astype(BF16)
    sent_high, sent_low = (
        lax.dot_general(onehot, jnp.concatenate(part, axis=1).astype(BF16), NT, preferred_element_type=F32)
        for part in (high_at, low_at)
    )
    send_ref[...] = jnp.zeros_like(send_ref)
    send_ref[:, :ranks] = (sent_high * 64.0 + sent_low).astype(jnp.int32)


def stage_table_kernel(after_ref, table_hbm, out_ref, arrived):
    del after_ref
    copy = pltpu.make_async_copy(table_hbm, out_ref, arrived)
    copy.start()
    copy.wait()


def fetch_kernel(capacity, asked_ref, table_ref, found_hbm, tiles_ref, tiles, table_f32, found_f32, found, moved, left):
    devices = asked_ref.shape[0]
    groups = left.shape[0]
    group = devices // groups
    turned = jnp.maximum(asked_ref[...].T[:capacity, :] - 1, 0)
    copies = []
    for place in range(groups):
        part = pl.ds(8 * place, 8)
        columns = slice(place * group, (place + 1) * group)
        tiles_ref[part, : capacity // 8 * group] = jnp.concatenate(
            [turned[rank : rank + 8, columns] for rank in range(0, capacity, 8)], axis=1
        )
        copies.append(pltpu.make_async_copy(tiles_ref.at[part], tiles.at[part], moved.at[place]))
        copies[-1].start()
    table_f32[...] = table_ref[...].astype(F32)
    results = []
    for place in range(groups):
        copies[place].wait()
        for device in range(group):
            for rank in range(capacity):
                row = tiles[8 * place + rank % 8, rank // 8 * group + device]
                target = (place * group + device) * capacity + rank
                found_f32[target : target + 1, :] = table_f32[pl.ds(row, 1), :]
        part = pl.ds(place * group * capacity, group * capacity)
        found[part, :] = found_f32[part, :].astype(BF16)
        results.append(pltpu.make_async_copy(found.at[part], found_hbm.at[part], left.at[place]))
        results[-1].start()
    for result in results:
        result.wait()


def forward_kernel(
    slot_ref, returned_ref, key_w_hbm, value_w_hbm, x_ref, c_ref, gain_ref,
    key_ref, value_ref, stat_ref, first_ref, last_ref, key_w_ref, value_w_ref,
    returned_f32, memory_f32, memory_ref, came,
):
    tokens, width = x_ref.shape
    chunk = 512
    weights = []
    for place in range(width // chunk):
        columns = pl.ds(place * chunk, chunk)
        for which, (source, weight) in enumerate(((key_w_hbm, key_w_ref), (value_w_hbm, value_w_ref))):
            weights.append(
                pltpu.make_async_copy(source.at[:, columns], weight.at[:, columns], came.at[2 * place + which])
            )
            weights[-1].start()
    lookups = slot_ref.shape[0]
    returned_f32[...] = returned_ref[...].astype(F32)
    unroll = 4

    def some_tokens(step, carry):
        for inner in range(unroll):
            token = step * unroll + inner
            for look in range(lookups):
                memory_f32[pl.ds(look * tokens + token, 1), :] = returned_f32[pl.ds(slot_ref[look, token], 1), :]
        return carry

    lax.fori_loop(0, tokens // unroll, some_tokens, 0)
    for look in range(lookups):
        memory_ref[:, look * LANES : (look + 1) * LANES] = memory_f32[look * tokens : (look + 1) * tokens, :].astype(BF16)
    memory = memory_ref[...]
    xx = kk = vv = xk = cv = jnp.zeros((tokens, LANES), F32)
    for start in range(0, width, chunk):
        weights[start // chunk * 2].wait()
        weights[start // chunk * 2 + 1].wait()
        key_ref[:, start : start + chunk] = jnp.dot(
            memory, key_w_ref[:, start : start + chunk], preferred_element_type=F32
        )
        value_ref[:, start : start + chunk] = jnp.dot(
            memory, value_w_ref[:, start : start + chunk], preferred_element_type=F32
        )
        for part in range(start, start + chunk, LANES):
            cols = slice(part, part + LANES)
            x = x_ref[:, cols].astype(F32)
            key = key_ref[:, cols]
            value = value_ref[:, cols]
            xx += x * x
            kk += key * key
            vv += value * value
            xk += x * key * gain_ref[:, cols]
            cv += c_ref[:, cols].astype(F32) * value
    xx, kk, vv, xk, cv = (jnp.sum(s, axis=-1, keepdims=True) for s in (xx, kk, vv, xk, cv))
    hidden_scale = lax.rsqrt(xx / width + EPSILON)
    key_scale = lax.rsqrt(kk / width + EPSILON)
    gate = jax.nn.sigmoid(hidden_scale * key_scale * xk / math.sqrt(width))
    conv_scale = lax.rsqrt(gate * gate * vv / width + EPSILON)
    for place, stat in enumerate((hidden_scale, key_scale, gate, conv_scale, xk, cv)):
        stat_ref[:, place : place + 1] = stat
    scaled = gate * conv_scale
    first_ref[...] = value_ref[:8, :] * scaled[:8]
    last_ref[...] = value_ref[tokens - 8 :, :] * scaled[tokens - 8 :]


def slope_of(conv_out):
    sigmoid = jax.nn.sigmoid(conv_out)
    return sigmoid * (1.0 + conv_out * (1.0 - sigmoid))


def alone_kernel(
    key_ref, value_ref, stat_ref, x_ref, c_ref, gain_ref, taps_ref, key_w_ref,
    conv_ref, back_ref, uv_ref, key_part_ref,
    conv_in, conv_grad, key_grad,
):
    tokens, width = value_ref.shape
    taps = taps_ref.shape[0]
    wide = (tokens, LANES)
    hidden_scale, key_scale, gate, conv_scale, xk = (stat_ref[:, i : i + 1] for i in range(5))
    scaled = jnp.broadcast_to(gate * conv_scale, wide)
    both = jnp.broadcast_to(hidden_scale * key_scale, wide)
    from_key = jnp.broadcast_to(hidden_scale * key_scale * key_scale * key_scale * xk / width, wide)
    for start in range(0, width, LANES):
        cols = slice(start, start + LANES)
        key_grad[:, cols] = (
            both * gain_ref[:, cols] * x_ref[:, cols].astype(F32) - from_key * key_ref[:, cols]
        ).astype(BF16)
    span = 256
    for start in range(0, key_part_ref.shape[1], span):
        rows = slice(start, start + span)
        key_part_ref[:, rows] = lax.dot_general(
            key_grad[...], key_w_ref[rows, :], NT, preferred_element_type=F32
        )
    conv_in[0:8, :] = jnp.zeros((8, LANES), F32)
    conv_grad[tokens:, :] = jnp.zeros((8, LANES), F32)
    uv_ref[...] = jnp.zeros(wide, F32)
    for start in range(0, width, LANES):
        cols = slice(start, start + LANES)
        conv_in[8:, :] = value_ref[:, cols] * scaled
        conv_out = taps_ref[0:1, cols] * conv_in[8:, :]
        for tap in range(1, taps):
            conv_out += taps_ref[tap : tap + 1, cols] * conv_in[8 - tap : 8 + tokens - tap, :]
        conv_ref[:, cols] = conv_out
        conv_grad[0:tokens, :] = c_ref[:, cols].astype(F32) * slope_of(conv_out)
        u = taps_ref[0:1, cols] * conv_grad[0:tokens, :]
        for tap in range(1, taps):
            u += taps_ref[tap : tap + 1, cols] * conv_grad[tap : tap + tokens, :]
        back_ref[:, cols] = u
        uv_ref[...] += u * value_ref[:, cols]


def finish_kernel(
    slot_ref, value_ref, stat_ref, c_ref, taps_ref, conv_ref, back_ref, uv_ref, key_part_ref,
    earlier_ref, later_ref, later_c_ref, value_w_ref,
    coef_hbm, head_hbm, grads_hbm,
    coef_ref, head_ref, sent, rim, rim_grad, rim_back, rim_uv, value_grad, memory_grad, slots, packed, left,
):
    tokens, width = value_ref.shape
    lookups = slot_ref.shape[0]
    taps = taps_ref.shape[0]
    seq = lax.axis_index("seq")
    has_earlier = jnp.where(seq > 0, 1.0, 0.0)
    has_later = jnp.where(seq < lax.axis_size("seq") - 1, 1.0, 0.0)
    hidden_scale, key_scale, gate, conv_scale, xk, cv = (stat_ref[:, i : i + 1] for i in range(6))
    scaled = gate * conv_scale
    last = slice(tokens - 8, tokens)
    rim_uv[...] = jnp.zeros_like(rim_uv)
    rim[8:16, :] = jnp.zeros((8, LANES), F32)
    rim_grad[0:8, :] = jnp.zeros((8, LANES), F32)
    rim_grad[16:24, :] = jnp.zeros((8, LANES), F32)
    slots[...] = jnp.zeros_like(slots)
    for start in range(0, width, LANES):
        cols = slice(start, start + LANES)
        weights = [taps_ref[tap : tap + 1, cols] for tap in range(taps)]
        alone = conv_ref[0:8, cols]
        rim[0:8, :] = earlier_ref[:, cols] * has_earlier
        joined = alone
        for tap in range(1, taps):
            joined += weights[tap] * rim[8 - tap : 16 - tap, :]
        head_ref[:, cols] = joined
        rim_grad[8:16, :] = c_ref[0:16, cols].astype(F32)[:8] * (slope_of(joined) - slope_of(alone))
        u = back_ref[0:8, cols]
        for tap in range(taps):
            u += weights[tap] * rim_grad[8 + tap : 16 + tap, :]
        rim_back[0:8, cols] = u
        rim_uv[0:8, :] += u * value_ref[0:8, cols]
        rim[16:24, :] = value_ref[last, cols] * scaled[last]
        rim[24:32, :] = later_ref[:, cols] * has_later
        beyond = weights[0] * rim[24:32, :]
        for tap in range(1, taps):
            beyond += weights[tap] * rim[24 - tap : 32 - tap, :]
        rim_grad[32:40, :] = later_c_ref[:, cols].astype(F32)[:8] * slope_of(beyond) * has_later
        u = back_ref[last, cols]
        rim_grad[24:32, :] = jnp.zeros((8, LANES), F32)
        for tap in range(1, taps):
            u += weights[tap] * rim_grad[24 + tap : 32 + tap, :]
        rim_back[8:16, cols] = u
        rim_uv[8:16, :] += u * value_ref[last, cols]
    uv = jnp.sum(
        jnp.concatenate([rim_uv[0:8, :], uv_ref[8 : tokens - 8, :], rim_uv[8:16, :]], axis=0), axis=-1, keepdims=True
    )
    cube = conv_scale * conv_scale * conv_scale
    gate_grad = cv + EPSILON * cube * uv
    score_grad = gate_grad * gate * (1.0 - gate) / math.sqrt(width)
    both = score_grad * hidden_scale * key_scale
    from_hidden = both * hidden_scale * hidden_scale * xk / width
    from_value = gate * gate * cube * uv / width
    coef_ref[:, 0:1] = both
    coef_ref[:, 1:2] = from_hidden
    coef_ref[:, 2:3] = gate
    small = [
        pltpu.make_async_copy(coef_ref, coef_hbm, sent.at[0]),
        pltpu.make_async_copy(head_ref, head_hbm, sent.at[1]),
    ]
    for copy in small:
        copy.start()
    wide = (tokens, LANES)
    score_w = jnp.broadcast_to(score_grad, wide)
    value_w = jnp.broadcast_to(gate * from_value, wide)
    scaled_w = jnp.broadcast_to(scaled, wide)
    gate_w = jnp.broadcast_to(gate, wide)
    for start in range(0, width, LANES):
        cols = slice(start, start + LANES)
        u = jnp.concatenate([rim_back[0:8, cols], back_ref[8 : tokens - 8, cols], rim_back[8:16, cols]], axis=0)
        value_grad[:, cols] = (
            gate_w * c_ref[:, cols].astype(F32) + scaled_w * u - value_w * value_ref[:, cols]
        ).astype(BF16)
    span = 256

    def place(looks):
        for look in looks:
            for token in range(tokens):
                slots[pl.ds(slot_ref[look, token], 1), :] = memory_grad[look * tokens + token : look * tokens + token + 1, :]

    done = range(0)
    for start in range(0, lookups * LANES, span):
        some = lax.dot_general(
            value_grad[...], value_w_ref[start : start + span, :], NT, preferred_element_type=F32
        )
        place(done)
        done = range(start // LANES, (start + span) // LANES)
        for look in done:
            cols = slice(look * LANES, (look + 1) * LANES)
            memory_grad[look * tokens : (look + 1) * tokens, :] = (
                some[:, look * LANES - start : (look + 1) * LANES - start] + score_w * key_part_ref[:, cols]
            )
    place(done)
    pieces = left.shape[0]
    rows = slots.shape[0] // pieces
    copies = []
    for piece in range(pieces):
        part = pl.ds(piece * rows, rows)
        packed[part, :] = slots[part, :].astype(BF16)
        copies.append(pltpu.make_async_copy(packed.at[part], grads_hbm.at[part], left.at[piece]))
        copies[-1].start()
    for copy in small + copies:
        copy.wait()


def outputs_kernel(key_ref, value_ref, coef_ref, x_ref, c_ref, gain_ref, conv_ref, head_ref, mixed_ref, hidden_ref):
    tokens, width = x_ref.shape
    both, own, gate = (jnp.broadcast_to(coef_ref[:, i : i + 1], (tokens, LANES)) for i in range(3))
    for start in range(0, width, LANES):
        cols = slice(start, start + LANES)
        x = x_ref[:, cols].astype(F32)
        conv_out = jnp.concatenate([head_ref[:, cols], conv_ref[8:, cols]], axis=0)
        mixed_ref[:, cols] = (x + conv_out * jax.nn.sigmoid(conv_out) + gate * value_ref[:, cols]).astype(BF16)
        hidden_ref[:, cols] = (
            c_ref[:, cols].astype(F32) + both * gain_ref[:, cols] * key_ref[:, cols] - own * x
        ).astype(BF16)


def add_kernel(capacity, tiles_ref, arrived_ref, out_hbm, tiles, moved, left, arrived, *totals):
    to_smem = pltpu.make_async_copy(tiles_ref, tiles, moved)
    to_smem.start()
    ways = len(totals)
    devices = arrived_ref.shape[0] // capacity
    group = devices * 8 // tiles_ref.shape[0]
    for total in totals:
        total[...] = jnp.zeros_like(total)
    arrived[...] = arrived_ref[...].astype(F32)
    to_smem.wait()
    for ranks in range(0, capacity, 8):

        def one_rank(inner, carry, ranks=ranks):
            for first in range(0, devices, ways):
                rows = [
                    tiles[device // group * 8 + inner, ranks // 8 * group + device % group]
                    for device in range(first, first + ways)
                ]
                sums = [
                    totals[way][pl.ds(rows[way], 1), :] + arrived[pl.ds(inner + ranks + (first + way) * capacity, 1), :]
                    for way in range(ways)
                ]
                for way in range(ways):
                    totals[way][pl.ds(rows[way], 1), :] = sums[way]
            return carry

        lax.fori_loop(0, 8, one_rank, 0)
    pieces = left.shape[0]
    each = out_hbm.shape[0] // pieces
    copies = []
    for piece in range(pieces):
        part = pl.ds(piece * each, each)
        sums = totals[0][part, :]
        for total in totals[1:]:
            sums = sums + total[part, :]
        totals[0][part, :] = sums
        copies.append(pltpu.make_async_copy(totals[0].at[part], out_hbm.at[part], left.at[piece]))
        copies[-1].start()
    for copy in copies:
        copy.wait()


def shards(
    hidden, row_ids, table, key_weight, value_weight, hidden_gain, key_gain, conv_gain, conv_kernel, cotangent
):
    tokens, width = hidden.shape[1:]
    lookups = row_ids.shape[2]
    rows_here, row_width = table.shape
    devices = lax.axis_size(("seq", "rows"))
    capacity = 3 * tokens * lookups // devices
    places = devices * capacity
    x, c = hidden[0], cotangent[0]
    gain = (hidden_gain * key_gain)[None]
    taps = conv_kernel * conv_gain[None]
    shape = jax.ShapeDtypeStruct

    send, slot_of = pl.pallas_call(
        functools.partial(route_kernel, rows_here, capacity),
        out_shape=(shape((devices, LANES), jnp.int32), shape((lookups, tokens), jnp.int32)),
        in_specs=[VMEM],
        out_specs=(VMEM, VMEM),
        name="route",
    )(row_ids[0].T)
    asked = exchange(send)
    table_here = pl.pallas_call(
        stage_table_kernel,
        out_shape=shape((rows_here, row_width), BF16),
        in_specs=[VMEM, ANY],
        out_specs=VMEM,
        scratch_shapes=[pltpu.SemaphoreType.DMA],
        compiler_params=params(4),
        cost_estimate=pl.CostEstimate(flops=places * row_width, bytes_accessed=6 * places * row_width, transcendentals=0),
        name="stage_table",
    )(slot_of, in_hbm(table))
    groups = 4
    found, tiles = pl.pallas_call(
        functools.partial(fetch_kernel, capacity),
        out_shape=(pltpu.HBM((places, row_width), BF16), shape((8 * groups, LANES), jnp.int32)),
        in_specs=[VMEM, VMEM],
        out_specs=(ANY, VMEM),
        scratch_shapes=[
            pltpu.SMEM((8 * groups, LANES), jnp.int32),
            pltpu.VMEM((rows_here, row_width), F32),
            pltpu.VMEM((places, row_width), F32),
            pltpu.VMEM((places, row_width), BF16),
            pltpu.SemaphoreType.DMA((groups,)),
            pltpu.SemaphoreType.DMA((groups,)),
        ],
        compiler_params=params(8),
        name="fetch",
    )(asked, table_here)
    returned = exchange(found.reshape(devices, capacity, row_width)).reshape(places, row_width)
    later_c = shifted(c[:16], "seq", -1)
    key, value, stats, first, last, key_w, value_w = pl.pallas_call(
        forward_kernel,
        out_shape=(
            shape((tokens, width), F32),
            shape((tokens, width), F32),
            shape((tokens, LANES), F32),
            shape((8, width), F32),
            shape((8, width), F32),
            shape(key_weight.shape, BF16),
            shape(value_weight.shape, BF16),
        ),
        in_specs=[SMEM, VMEM, ANY, ANY, VMEM, VMEM, VMEM],
        out_specs=(VMEM,) * 7,
        scratch_shapes=[
            pltpu.VMEM((places, row_width), F32),
            pltpu.VMEM((tokens * lookups, row_width), F32),
            pltpu.VMEM((tokens, lookups * row_width), BF16),
            pltpu.SemaphoreType.DMA((width // 256,)),
        ],
        compiler_params=params(8),
        name="forward",
    )(slot_of, returned, in_hbm(key_weight), in_hbm(value_weight), x, c, gain)
    earlier = shifted(last, "seq", 1)
    later = shifted(first, "seq", -1)
    conv_out, back, uv, key_part = pl.pallas_call(
        alone_kernel,
        out_shape=(
            shape((tokens, width), F32),
            shape((tokens, width), F32),
            shape((tokens, LANES), F32),
            shape((tokens, lookups * row_width), F32),
        ),
        in_specs=[VMEM] * 8,
        out_specs=(VMEM,) * 4,
        scratch_shapes=[
            pltpu.VMEM((tokens + 8, LANES), F32),
            pltpu.VMEM((tokens + 8, LANES), F32),
            pltpu.VMEM((tokens, width), BF16),
        ],
        compiler_params=params(4),
        cost_estimate=pl.CostEstimate(
            flops=40 * tokens * width, bytes_accessed=4 * key_weight.size, transcendentals=2 * tokens * width
        ),
        name="alone",
    )(key, value, stats, x, c, gain, taps, key_w)
    coef, head, grads = pl.pallas_call(
        finish_kernel,
        out_shape=(
            pltpu.HBM((tokens, LANES), F32),
            pltpu.HBM((8, width), F32),
            pltpu.HBM((places, row_width), BF16),
        ),
        in_specs=[SMEM] + [VMEM] * 12,
        out_specs=(ANY,) * 3,
        scratch_shapes=[
            pltpu.VMEM((tokens, LANES), F32),
            pltpu.VMEM((8, width), F32),
            pltpu.SemaphoreType.DMA((2,)),
            pltpu.VMEM((32, LANES), F32),
            pltpu.VMEM((40, LANES), F32),
            pltpu.VMEM((16, width), F32),
            pltpu.VMEM((16, LANES), F32),
            pltpu.VMEM((tokens, width), BF16),
            pltpu.VMEM((tokens * lookups, row_width), F32),
            pltpu.VMEM((places, row_width), F32),
            pltpu.VMEM((places, row_width), BF16),
            pltpu.SemaphoreType.DMA((4,)),
        ],
        compiler_params=params(12),
        name="finish",
    )(slot_of, value, stats, c, taps, conv_out, back, uv, key_part, earlier, later, later_c, value_w)
    arrived = exchange(grads.reshape(devices, capacity, row_width)).reshape(places, row_width)
    mixed, hidden_grad = pl.pallas_call(
        outputs_kernel,
        out_shape=(shape((tokens, width), BF16), shape((tokens, width), BF16)),
        in_specs=[VMEM] * 8,
        out_specs=(VMEM, VMEM),
        cost_estimate=pl.CostEstimate(
            flops=10 * tokens * width, bytes_accessed=20 * tokens * width, transcendentals=tokens * width
        ),
        name="outputs",
    )(key, value, coef, x, c, gain, conv_out, head)
    ways = 8
    table_grad = pl.pallas_call(
        functools.partial(add_kernel, capacity),
        out_shape=pltpu.HBM((rows_here, row_width), F32),
        in_specs=[VMEM, VMEM],
        out_specs=ANY,
        scratch_shapes=[
            pltpu.SMEM((8 * groups, LANES), jnp.int32),
            pltpu.SemaphoreType.DMA,
            pltpu.SemaphoreType.DMA((4,)),
            pltpu.VMEM((places, row_width), F32),
        ]
        + [pltpu.VMEM((rows_here, row_width), F32)] * ways,
        compiler_params=params(24),
        name="add",
    )(tiles, arrived)
    return (mixed[None], hidden_grad[None], table_grad)


def solution(mesh):
    seq_block = P("rows", "seq", None)
    table_block = P(("seq", "rows"), None)
    return jax.shard_map(
        shards,
        mesh=mesh,
        in_specs=(seq_block, seq_block, table_block, P(), P(), P(), P(), P(), P(), seq_block),
        out_specs=(seq_block, seq_block, table_block),
        check_vma=False,
    )
```

```python
import functools
import math

import jax
import jax.numpy as jnp
from jax import lax
from jax.experimental import pallas as pl
from jax.experimental.pallas import tpu as pltpu
from jax.sharding import PartitionSpec as P

EPSILON = 1e-06
F32 = jnp.float32
BF16 = jnp.bfloat16
LANES = 128
NT = (((1,), (1,)), ((), ()))
VMEM = pl.BlockSpec(memory_space=pltpu.VMEM)
SMEM = pl.BlockSpec(memory_space=pltpu.SMEM)
ANY = pl.BlockSpec(memory_space=pl.ANY)


def params(mib):
    return pltpu.CompilerParams(vmem_limit_bytes=mib << 20)


def in_hbm(x):
    return pltpu.with_memory_space_constraint(x, pltpu.HBM)


def in_vmem(x):
    return pltpu.with_memory_space_constraint(x, pltpu.VMEM)


def shifted(block, axis, distance):
    devices = lax.axis_size(axis)
    return lax.ppermute(block, axis, [(i, (i + distance) % devices) for i in range(devices)])


def exchange(block):
    return lax.all_to_all(block, ("seq", "rows"), split_axis=0, concat_axis=0, tiled=True)


def route_kernel(rows_here, capacity, ids_ref, send_ref, slot_ref):
    lookups, tokens = ids_ref.shape
    owners = send_ref.shape[0]
    ids = ids_ref[...]
    shift = rows_here.bit_length() - 1
    owner_of = lax.shift_right_logical(ids, shift)
    code = (ids & (rows_here - 1)) + 1
    high = lax.shift_right_logical(code, 6).astype(F32)
    low = (code & 63).astype(F32)
    owner_axis = lax.broadcasted_iota(jnp.int32, (owners, tokens), 0)
    source = lax.broadcasted_iota(jnp.int32, (tokens, 2 * tokens), 0)
    target = lax.broadcasted_iota(jnp.int32, (tokens, 2 * tokens), 1)
    earlier = jnp.where(source < target, 1.0, 0.0).astype(BF16)
    ranks = 32
    rank_axis = lax.broadcasted_iota(jnp.int32, (ranks, tokens), 0)
    onehots = [jnp.where(owner_axis == owner_of[look : look + 1, :], 1.0, 0.0) for look in range(lookups)]
    counts = jnp.dot(jnp.concatenate(onehots, axis=0).astype(BF16), earlier, preferred_element_type=F32)
    base = jnp.zeros((owners, tokens), F32)
    high_at, low_at = [], []
    for look in range(lookups):
        here = counts[look * owners : (look + 1) * owners]
        rank = jnp.sum(onehots[look] * (here[:, :tokens] + base), axis=0, keepdims=True).astype(jnp.int32)
        base = base + here[:, tokens:]
        slot_ref[look : look + 1, :] = owner_of[look : look + 1, :] * capacity + rank
        at_rank = rank_axis == rank
        high_at.append(jnp.where(at_rank, high[look : look + 1, :], 0.0))
        low_at.append(jnp.where(at_rank, low[look : look + 1, :], 0.0))
    onehot = jnp.concatenate(onehots, axis=1).astype(BF16)
    sent_high, sent_low = (
        lax.dot_general(onehot, jnp.concatenate(part, axis=1).astype(BF16), NT, preferred_element_type=F32)
        for part in (high_at, low_at)
    )
    send_ref[...] = jnp.zeros_like(send_ref)
    send_ref[:, :ranks] = (sent_high * 64.0 + sent_low).astype(jnp.int32)


def stage_table_kernel(after_ref, table_hbm, out_ref, arrived):
    del after_ref
    copy = pltpu.make_async_copy(table_hbm, out_ref, arrived)
    copy.start()
    copy.wait()


def fetch_kernel(capacity, asked_ref, table_ref, found_hbm, tiles_ref, tiles, table_f32, found_f32, found, moved, left):
    devices = asked_ref.shape[0]
    groups = left.shape[0]
    group = devices // groups
    turned = jnp.maximum(asked_ref[...].T[:capacity, :] - 1, 0)
    copies = []
    for place in range(groups):
        part = pl.ds(8 * place, 8)
        columns = slice(place * group, (place + 1) * group)
        tiles_ref[part, : capacity // 8 * group] = jnp.concatenate(
            [turned[rank : rank + 8, columns] for rank in range(0, capacity, 8)], axis=1
        )
        copies.append(pltpu.make_async_copy(tiles_ref.at[part], tiles.at[part], moved.at[place]))
        copies[-1].start()
    table_f32[...] = table_ref[...].astype(F32)
    results = []
    for place in range(groups):
        copies[place].wait()
        for device in range(group):
            for rank in range(capacity):
                row = tiles[8 * place + rank % 8, rank // 8 * group + device]
                target = (place * group + device) * capacity + rank
                found_f32[target : target + 1, :] = table_f32[pl.ds(row, 1), :]
        part = pl.ds(place * group * capacity, group * capacity)
        found[part, :] = found_f32[part, :].astype(BF16)
        results.append(pltpu.make_async_copy(found.at[part], found_hbm.at[part], left.at[place]))
        results[-1].start()
    for result in results:
        result.wait()


def forward_kernel(
    slot_ref, returned_ref, key_w_hbm, value_w_hbm, x_ref, c_ref, gain_ref,
    key_ref, value_ref, stat_ref, first_ref, last_ref, key_w_ref, value_w_ref,
    slots, returned_f32, memory_f32, memory_ref, came, slots_came,
):
    tokens, width = x_ref.shape
    to_smem = pltpu.make_async_copy(slot_ref, slots, slots_came)
    to_smem.start()
    chunk = 256
    weights = []
    for place in range(width // chunk):
        columns = pl.ds(place * chunk, chunk)
        for which, (source, weight) in enumerate(((key_w_hbm, key_w_ref), (value_w_hbm, value_w_ref))):
            weights.append(
                pltpu.make_async_copy(source.at[:, columns], weight.at[:, columns], came.at[2 * place + which])
            )
            weights[-1].start()
    lookups = slot_ref.shape[0]
    returned_f32[...] = returned_ref[...].astype(F32)
    to_smem.wait()
    for look in range(lookups):
        for token in range(tokens):
            target = look * tokens + token
            memory_f32[target : target + 1, :] = returned_f32[pl.ds(slots[look, token], 1), :]
    for look in range(lookups):
        memory_ref[:, look * LANES : (look + 1) * LANES] = memory_f32[look * tokens : (look + 1) * tokens, :].astype(BF16)
    memory = memory_ref[...]
    xx = kk = vv = xk = cv = jnp.zeros((tokens, LANES), F32)
    for start in range(0, width, chunk):
        weights[start // chunk * 2].wait()
        weights[start // chunk * 2 + 1].wait()
        key_ref[:, start : start + chunk] = jnp.dot(
            memory, key_w_ref[:, start : start + chunk], preferred_element_type=F32
        )
        value_ref[:, start : start + chunk] = jnp.dot(
            memory, value_w_ref[:, start : start + chunk], preferred_element_type=F32
        )
        for part in range(start, start + chunk, LANES):
            cols = slice(part, part + LANES)
            x = x_ref[:, cols].astype(F32)
            key = key_ref[:, cols]
            value = value_ref[:, cols]
            xx += x * x
            kk += key * key
            vv += value * value
            xk += x * key * gain_ref[:, cols]
            cv += c_ref[:, cols].astype(F32) * value
    xx, kk, vv, xk, cv = (jnp.sum(s, axis=-1, keepdims=True) for s in (xx, kk, vv, xk, cv))
    hidden_scale = lax.rsqrt(xx / width + EPSILON)
    key_scale = lax.rsqrt(kk / width + EPSILON)
    gate = jax.nn.sigmoid(hidden_scale * key_scale * xk / math.sqrt(width))
    conv_scale = lax.rsqrt(gate * gate * vv / width + EPSILON)
    for place, stat in enumerate((hidden_scale, key_scale, gate, conv_scale, xk, cv)):
        stat_ref[:, place : place + 1] = stat
    scaled = gate * conv_scale
    first_ref[...] = value_ref[:8, :] * scaled[:8]
    last_ref[...] = value_ref[tokens - 8 :, :] * scaled[tokens - 8 :]


def slope_of(conv_out):
    sigmoid = jax.nn.sigmoid(conv_out)
    return sigmoid * (1.0 + conv_out * (1.0 - sigmoid))


def alone_kernel(
    key_ref, value_ref, stat_ref, x_ref, c_ref, gain_ref, taps_ref, key_w_ref,
    conv_ref, back_ref, uv_ref, key_part_ref,
    conv_in, conv_grad, key_grad,
):
    tokens, width = value_ref.shape
    taps = taps_ref.shape[0]
    wide = (tokens, LANES)
    hidden_scale, key_scale, gate, conv_scale, xk = (stat_ref[:, i : i + 1] for i in range(5))
    scaled = jnp.broadcast_to(gate * conv_scale, wide)
    both = jnp.broadcast_to(hidden_scale * key_scale, wide)
    from_key = jnp.broadcast_to(hidden_scale * key_scale * key_scale * key_scale * xk / width, wide)
    for start in range(0, width, LANES):
        cols = slice(start, start + LANES)
        key_grad[:, cols] = (
            both * gain_ref[:, cols] * x_ref[:, cols].astype(F32) - from_key * key_ref[:, cols]
        ).astype(BF16)
    span = 256
    for start in range(0, key_part_ref.shape[1], span):
        rows = slice(start, start + span)
        key_part_ref[:, rows] = lax.dot_general(
            key_grad[...], key_w_ref[rows, :], NT, preferred_element_type=F32
        )
    conv_in[0:8, :] = jnp.zeros((8, LANES), F32)
    conv_grad[tokens:, :] = jnp.zeros((8, LANES), F32)
    uv_ref[...] = jnp.zeros(wide, F32)
    for start in range(0, width, LANES):
        cols = slice(start, start + LANES)
        conv_in[8:, :] = value_ref[:, cols] * scaled
        conv_out = taps_ref[0:1, cols] * conv_in[8:, :]
        for tap in range(1, taps):
            conv_out += taps_ref[tap : tap + 1, cols] * conv_in[8 - tap : 8 + tokens - tap, :]
        conv_ref[:, cols] = conv_out
        conv_grad[0:tokens, :] = c_ref[:, cols].astype(F32) * slope_of(conv_out)
        u = taps_ref[0:1, cols] * conv_grad[0:tokens, :]
        for tap in range(1, taps):
            u += taps_ref[tap : tap + 1, cols] * conv_grad[tap : tap + tokens, :]
        back_ref[:, cols] = u
        uv_ref[...] += u * value_ref[:, cols]


def finish_kernel(
    slot_ref, value_ref, stat_ref, c_ref, taps_ref, conv_ref, back_ref, uv_ref, key_part_ref,
    earlier_ref, later_ref, later_c_ref, value_w_ref,
    coef_hbm, head_hbm, grads_hbm,
    coef_ref, head_ref, sent, rim, rim_grad, rim_back, rim_uv, value_grad, memory_grad, slots, packed, left, slot_of, slots_came,
):
    to_smem = pltpu.make_async_copy(slot_ref, slot_of, slots_came)
    to_smem.start()
    tokens, width = value_ref.shape
    lookups = slot_ref.shape[0]
    taps = taps_ref.shape[0]
    seq = lax.axis_index("seq")
    has_earlier = jnp.where(seq > 0, 1.0, 0.0)
    has_later = jnp.where(seq < lax.axis_size("seq") - 1, 1.0, 0.0)
    hidden_scale, key_scale, gate, conv_scale, xk, cv = (stat_ref[:, i : i + 1] for i in range(6))
    scaled = gate * conv_scale
    last = slice(tokens - 8, tokens)
    rim_uv[...] = jnp.zeros_like(rim_uv)
    rim[8:16, :] = jnp.zeros((8, LANES), F32)
    rim_grad[0:8, :] = jnp.zeros((8, LANES), F32)
    rim_grad[16:24, :] = jnp.zeros((8, LANES), F32)
    slots[...] = jnp.zeros_like(slots)
    for start in range(0, width, LANES):
        cols = slice(start, start + LANES)
        weights = [taps_ref[tap : tap + 1, cols] for tap in range(taps)]
        alone = conv_ref[0:8, cols]
        rim[0:8, :] = earlier_ref[:, cols] * has_earlier
        joined = alone
        for tap in range(1, taps):
            joined += weights[tap] * rim[8 - tap : 16 - tap, :]
        head_ref[:, cols] = joined
        rim_grad[8:16, :] = c_ref[0:16, cols].astype(F32)[:8] * (slope_of(joined) - slope_of(alone))
        u = back_ref[0:8, cols]
        for tap in range(taps):
            u += weights[tap] * rim_grad[8 + tap : 16 + tap, :]
        rim_back[0:8, cols] = u
        rim_uv[0:8, :] += u * value_ref[0:8, cols]
        rim[16:24, :] = value_ref[last, cols] * scaled[last]
        rim[24:32, :] = later_ref[:, cols] * has_later
        beyond = weights[0] * rim[24:32, :]
        for tap in range(1, taps):
            beyond += weights[tap] * rim[24 - tap : 32 - tap, :]
        rim_grad[32:40, :] = later_c_ref[:, cols].astype(F32)[:8] * slope_of(beyond) * has_later
        u = back_ref[last, cols]
        rim_grad[24:32, :] = jnp.zeros((8, LANES), F32)
        for tap in range(1, taps):
            u += weights[tap] * rim_grad[24 + tap : 32 + tap, :]
        rim_back[8:16, cols] = u
        rim_uv[8:16, :] += u * value_ref[last, cols]
    uv = jnp.sum(
        jnp.concatenate([rim_uv[0:8, :], uv_ref[8 : tokens - 8, :], rim_uv[8:16, :]], axis=0), axis=-1, keepdims=True
    )
    cube = conv_scale * conv_scale * conv_scale
    gate_grad = cv + EPSILON * cube * uv
    score_grad = gate_grad * gate * (1.0 - gate) / math.sqrt(width)
    both = score_grad * hidden_scale * key_scale
    from_hidden = both * hidden_scale * hidden_scale * xk / width
    from_value = gate * gate * cube * uv / width
    coef_ref[:, 0:1] = both
    coef_ref[:, 1:2] = from_hidden
    coef_ref[:, 2:3] = gate
    small = [
        pltpu.make_async_copy(coef_ref, coef_hbm, sent.at[0]),
        pltpu.make_async_copy(head_ref, head_hbm, sent.at[1]),
    ]
    for copy in small:
        copy.start()
    wide = (tokens, LANES)
    score_w = jnp.broadcast_to(score_grad, wide)
    value_w = jnp.broadcast_to(gate * from_value, wide)
    scaled_w = jnp.broadcast_to(scaled, wide)
    gate_w = jnp.broadcast_to(gate, wide)
    for start in range(0, width, LANES):
        cols = slice(start, start + LANES)
        u = jnp.concatenate([rim_back[0:8, cols], back_ref[8 : tokens - 8, cols], rim_back[8:16, cols]], axis=0)
        value_grad[:, cols] = (
            gate_w * c_ref[:, cols].astype(F32) + scaled_w * u - value_w * value_ref[:, cols]
        ).astype(BF16)
    span = 256

    def place(looks):
        for look in looks:
            for token in range(tokens):
                slots[pl.ds(slot_of[look, token], 1), :] = memory_grad[look * tokens + token : look * tokens + token + 1, :]

    to_smem.wait()
    done = range(0)
    for start in range(0, lookups * LANES, span):
        some = lax.dot_general(
            value_grad[...], value_w_ref[start : start + span, :], NT, preferred_element_type=F32
        )
        place(done)
        done = range(start // LANES, (start + span) // LANES)
        for look in done:
            cols = slice(look * LANES, (look + 1) * LANES)
            memory_grad[look * tokens : (look + 1) * tokens, :] = (
                some[:, look * LANES - start : (look + 1) * LANES - start] + score_w * key_part_ref[:, cols]
            )
    place(done)
    pieces = left.shape[0]
    rows = slots.shape[0] // pieces
    copies = []
    for piece in range(pieces):
        part = pl.ds(piece * rows, rows)
        packed[part, :] = slots[part, :].astype(BF16)
        copies.append(pltpu.make_async_copy(packed.at[part], grads_hbm.at[part], left.at[piece]))
        copies[-1].start()
    for copy in small + copies:
        copy.wait()


def outputs_kernel(key_ref, value_ref, coef_ref, x_ref, c_ref, gain_ref, conv_ref, head_ref, mixed_ref, hidden_ref):
    tokens, width = x_ref.shape
    both, own, gate = (jnp.broadcast_to(coef_ref[:, i : i + 1], (tokens, LANES)) for i in range(3))
    for start in range(0, width, LANES):
        cols = slice(start, start + LANES)
        x = x_ref[:, cols].astype(F32)
        conv_out = jnp.concatenate([head_ref[:, cols], conv_ref[8:, cols]], axis=0)
        mixed_ref[:, cols] = (x + conv_out * jax.nn.sigmoid(conv_out) + gate * value_ref[:, cols]).astype(BF16)
        hidden_ref[:, cols] = (
            c_ref[:, cols].astype(F32) + both * gain_ref[:, cols] * key_ref[:, cols] - own * x
        ).astype(BF16)


def add_kernel(capacity, tiles_ref, arrived_ref, out_hbm, tiles, moved, left, arrived, *totals):
    to_smem = pltpu.make_async_copy(tiles_ref, tiles, moved)
    to_smem.start()
    ways = len(totals)
    devices = arrived_ref.shape[0] // capacity
    group = devices * 8 // tiles_ref.shape[0]
    for total in totals:
        total[...] = jnp.zeros_like(total)
    arrived[...] = arrived_ref[...].astype(F32)
    to_smem.wait()
    for ranks in range(0, capacity, 8):

        def one_rank(inner, carry, ranks=ranks):
            for first in range(0, devices, ways):
                rows = [
                    tiles[device // group * 8 + inner, ranks // 8 * group + device % group]
                    for device in range(first, first + ways)
                ]
                sums = [
                    totals[way][pl.ds(rows[way], 1), :] + arrived[pl.ds(inner + ranks + (first + way) * capacity, 1), :]
                    for way in range(ways)
                ]
                for way in range(ways):
                    totals[way][pl.ds(rows[way], 1), :] = sums[way]
            return carry

        lax.fori_loop(0, 8, one_rank, 0)
    pieces = left.shape[0]
    each = out_hbm.shape[0] // pieces
    copies = []
    for piece in range(pieces):
        part = pl.ds(piece * each, each)
        sums = totals[0][part, :]
        for total in totals[1:]:
            sums = sums + total[part, :]
        totals[0][part, :] = sums
        copies.append(pltpu.make_async_copy(totals[0].at[part], out_hbm.at[part], left.at[piece]))
        copies[-1].start()
    for copy in copies:
        copy.wait()


def shards(
    hidden, row_ids, table, key_weight, value_weight, hidden_gain, key_gain, conv_gain, conv_kernel, cotangent
):
    tokens, width = hidden.shape[1:]
    lookups = row_ids.shape[2]
    rows_here, row_width = table.shape
    devices = lax.axis_size(("seq", "rows"))
    capacity = 3 * tokens * lookups // devices
    places = devices * capacity
    x, c = hidden[0], cotangent[0]
    gain = (hidden_gain * key_gain)[None]
    taps = conv_kernel * conv_gain[None]
    shape = jax.ShapeDtypeStruct

    send, slot_of = pl.pallas_call(
        functools.partial(route_kernel, rows_here, capacity),
        out_shape=(shape((devices, LANES), jnp.int32), shape((lookups, tokens), jnp.int32)),
        in_specs=[VMEM],
        out_specs=(VMEM, VMEM),
        name="route",
    )(row_ids[0].T)
    asked = exchange(send)
    table_here = pl.pallas_call(
        stage_table_kernel,
        out_shape=shape((rows_here, row_width), BF16),
        in_specs=[VMEM, ANY],
        out_specs=VMEM,
        scratch_shapes=[pltpu.SemaphoreType.DMA],
        compiler_params=params(4),
        cost_estimate=pl.CostEstimate(flops=places * row_width, bytes_accessed=6 * places * row_width, transcendentals=0),
        name="stage_table",
    )(slot_of, in_hbm(table))
    groups = 4
    found, tiles = pl.pallas_call(
        functools.partial(fetch_kernel, capacity),
        out_shape=(pltpu.HBM((places, row_width), BF16), shape((8 * groups, LANES), jnp.int32)),
        in_specs=[VMEM, VMEM],
        out_specs=(ANY, VMEM),
        scratch_shapes=[
            pltpu.SMEM((8 * groups, LANES), jnp.int32),
            pltpu.VMEM((rows_here, row_width), F32),
            pltpu.VMEM((places, row_width), F32),
            pltpu.VMEM((places, row_width), BF16),
            pltpu.SemaphoreType.DMA((groups,)),
            pltpu.SemaphoreType.DMA((groups,)),
        ],
        compiler_params=params(8),
        name="fetch",
    )(asked, table_here)
    returned = exchange(found.reshape(devices, capacity, row_width)).reshape(places, row_width)
    later_c = shifted(c[:16], "seq", -1)
    key, value, stats, first, last, key_w, value_w = pl.pallas_call(
        forward_kernel,
        out_shape=(
            shape((tokens, width), F32),
            shape((tokens, width), F32),
            shape((tokens, LANES), F32),
            shape((8, width), F32),
            shape((8, width), F32),
            shape(key_weight.shape, BF16),
            shape(value_weight.shape, BF16),
        ),
        in_specs=[VMEM, VMEM, ANY, ANY, VMEM, VMEM, VMEM],
        out_specs=(VMEM,) * 7,
        scratch_shapes=[
            pltpu.SMEM((lookups, tokens), jnp.int32),
            pltpu.VMEM((places, row_width), F32),
            pltpu.VMEM((tokens * lookups, row_width), F32),
            pltpu.VMEM((tokens, lookups * row_width), BF16),
            pltpu.SemaphoreType.DMA((width // 128,)),
            pltpu.SemaphoreType.DMA,
        ],
        compiler_params=params(8),
        name="forward",
    )(slot_of, returned, in_hbm(key_weight), in_hbm(value_weight), x, c, gain)
    earlier = shifted(last, "seq", 1)
    later = shifted(first, "seq", -1)
    conv_out, back, uv, key_part = pl.pallas_call(
        alone_kernel,
        out_shape=(
            shape((tokens, width), F32),
            shape((tokens, width), F32),
            shape((tokens, LANES), F32),
            shape((tokens, lookups * row_width), F32),
        ),
        in_specs=[VMEM] * 8,
        out_specs=(VMEM,) * 4,
        scratch_shapes=[
            pltpu.VMEM((tokens + 8, LANES), F32),
            pltpu.VMEM((tokens + 8, LANES), F32),
            pltpu.VMEM((tokens, width), BF16),
        ],
        compiler_params=params(4),
        cost_estimate=pl.CostEstimate(
            flops=40 * tokens * width, bytes_accessed=4 * key_weight.size, transcendentals=2 * tokens * width
        ),
        name="alone",
    )(key, value, stats, x, c, gain, taps, key_w)
    coef, head, grads = pl.pallas_call(
        finish_kernel,
        out_shape=(
            pltpu.HBM((tokens, LANES), F32),
            pltpu.HBM((8, width), F32),
            pltpu.HBM((places, row_width), BF16),
        ),
        in_specs=[VMEM] * 13,
        out_specs=(ANY,) * 3,
        scratch_shapes=[
            pltpu.VMEM((tokens, LANES), F32),
            pltpu.VMEM((8, width), F32),
            pltpu.SemaphoreType.DMA((2,)),
            pltpu.VMEM((32, LANES), F32),
            pltpu.VMEM((40, LANES), F32),
            pltpu.VMEM((16, width), F32),
            pltpu.VMEM((16, LANES), F32),
            pltpu.VMEM((tokens, width), BF16),
            pltpu.VMEM((tokens * lookups, row_width), F32),
            pltpu.VMEM((places, row_width), F32),
            pltpu.VMEM((places, row_width), BF16),
            pltpu.SemaphoreType.DMA((4,)),
            pltpu.SMEM((lookups, tokens), jnp.int32),
            pltpu.SemaphoreType.DMA,
        ],
        compiler_params=params(12),
        name="finish",
    )(slot_of, value, stats, c, taps, conv_out, back, uv, key_part, earlier, later, later_c, value_w)
    arrived = exchange(grads.reshape(devices, capacity, row_width)).reshape(places, row_width)
    mixed, hidden_grad = pl.pallas_call(
        outputs_kernel,
        out_shape=(shape((tokens, width), BF16), shape((tokens, width), BF16)),
        in_specs=[VMEM] * 8,
        out_specs=(VMEM, VMEM),
        cost_estimate=pl.CostEstimate(
            flops=10 * tokens * width, bytes_accessed=20 * tokens * width, transcendentals=tokens * width
        ),
        name="outputs",
    )(key, value, coef, x, c, gain, conv_out, head)
    ways = 8
    table_grad = pl.pallas_call(
        functools.partial(add_kernel, capacity),
        out_shape=pltpu.HBM((rows_here, row_width), F32),
        in_specs=[VMEM, VMEM],
        out_specs=ANY,
        scratch_shapes=[
            pltpu.SMEM((8 * groups, LANES), jnp.int32),
            pltpu.SemaphoreType.DMA,
            pltpu.SemaphoreType.DMA((4,)),
            pltpu.VMEM((places, row_width), F32),
        ]
        + [pltpu.VMEM((rows_here, row_width), F32)] * ways,
        compiler_params=params(24),
        name="add",
    )(tiles, arrived)
    return (mixed[None], hidden_grad[None], table_grad)


def solution(mesh):
    seq_block = P("rows", "seq", None)
    table_block = P(("seq", "rows"), None)
    return jax.shard_map(
        shards,
        mesh=mesh,
        in_specs=(seq_block, seq_block, table_block, P(), P(), P(), P(), P(), P(), seq_block),
        out_specs=(seq_block, seq_block, table_block),
        check_vma=False,
    )
```

```python
import functools
import math

import jax
import jax.numpy as jnp
from jax import lax
from jax.experimental import pallas as pl
from jax.experimental.pallas import tpu as pltpu
from jax.sharding import PartitionSpec as P

EPSILON = 1e-06
F32 = jnp.float32
BF16 = jnp.bfloat16
LANES = 128
NT = (((1,), (1,)), ((), ()))
VMEM = pl.BlockSpec(memory_space=pltpu.VMEM)
SMEM = pl.BlockSpec(memory_space=pltpu.SMEM)
ANY = pl.BlockSpec(memory_space=pl.ANY)


def params(mib):
    return pltpu.CompilerParams(vmem_limit_bytes=mib << 20)


def in_hbm(x):
    return pltpu.with_memory_space_constraint(x, pltpu.HBM)


def in_vmem(x):
    return pltpu.with_memory_space_constraint(x, pltpu.VMEM)


def shifted(block, axis, distance):
    devices = lax.axis_size(axis)
    return lax.ppermute(block, axis, [(i, (i + distance) % devices) for i in range(devices)])


def exchange(block):
    return lax.all_to_all(block, ("seq", "rows"), split_axis=0, concat_axis=0, tiled=True)


def route_kernel(rows_here, capacity, ids_ref, send_ref, slot_ref):
    lookups, tokens = ids_ref.shape
    owners = send_ref.shape[0]
    ids = ids_ref[...]
    shift = rows_here.bit_length() - 1
    owner_of = lax.shift_right_logical(ids, shift)
    code = (ids & (rows_here - 1)) + 1
    high = lax.shift_right_logical(code, 6).astype(F32)
    low = (code & 63).astype(F32)
    owner_axis = lax.broadcasted_iota(jnp.int32, (owners, tokens), 0)
    source = lax.broadcasted_iota(jnp.int32, (tokens, 2 * tokens), 0)
    target = lax.broadcasted_iota(jnp.int32, (tokens, 2 * tokens), 1)
    earlier = jnp.where(source < target, 1.0, 0.0).astype(BF16)
    ranks = 32
    rank_axis = lax.broadcasted_iota(jnp.int32, (ranks, tokens), 0)
    onehots = [jnp.where(owner_axis == owner_of[look : look + 1, :], 1.0, 0.0) for look in range(lookups)]
    counts = jnp.dot(jnp.concatenate(onehots, axis=0).astype(BF16), earlier, preferred_element_type=F32)
    base = jnp.zeros((owners, tokens), F32)
    high_at, low_at = [], []
    for look in range(lookups):
        here = counts[look * owners : (look + 1) * owners]
        rank = jnp.sum(onehots[look] * (here[:, :tokens] + base), axis=0, keepdims=True).astype(jnp.int32)
        base = base + here[:, tokens:]
        slot_ref[look : look + 1, :] = owner_of[look : look + 1, :] * capacity + rank
        at_rank = rank_axis == rank
        high_at.append(jnp.where(at_rank, high[look : look + 1, :], 0.0))
        low_at.append(jnp.where(at_rank, low[look : look + 1, :], 0.0))
    onehot = jnp.concatenate(onehots, axis=1).astype(BF16)
    sent_high, sent_low = (
        lax.dot_general(onehot, jnp.concatenate(part, axis=1).astype(BF16), NT, preferred_element_type=F32)
        for part in (high_at, low_at)
    )
    send_ref[...] = jnp.zeros_like(send_ref)
    send_ref[:, :ranks] = (sent_high * 64.0 + sent_low).astype(jnp.int32)


def stage_table_kernel(after_ref, table_hbm, out_ref, arrived):
    del after_ref
    copy = pltpu.make_async_copy(table_hbm, out_ref, arrived)
    copy.start()
    copy.wait()


def fetch_kernel(capacity, asked_ref, table_ref, found_hbm, tiles_ref, tiles, table_f32, found_f32, found, moved, left):
    devices = asked_ref.shape[0]
    groups = left.shape[0]
    group = devices // groups
    turned = jnp.maximum(asked_ref[...].T[:capacity, :] - 1, 0)
    copies = []
    for place in range(groups):
        part = pl.ds(8 * place, 8)
        columns = slice(place * group, (place + 1) * group)
        tiles_ref[part, : capacity // 8 * group] = jnp.concatenate(
            [turned[rank : rank + 8, columns] for rank in range(0, capacity, 8)], axis=1
        )
        copies.append(pltpu.make_async_copy(tiles_ref.at[part], tiles.at[part], moved.at[place]))
        copies[-1].start()
    table_f32[...] = table_ref[...].astype(F32)
    results = []
    for place in range(groups):
        copies[place].wait()
        for device in range(group):
            for rank in range(capacity):
                row = tiles[8 * place + rank % 8, rank // 8 * group + device]
                target = (place * group + device) * capacity + rank
                found_f32[target : target + 1, :] = table_f32[pl.ds(row, 1), :]
        part = pl.ds(place * group * capacity, group * capacity)
        found[part, :] = found_f32[part, :].astype(BF16)
        results.append(pltpu.make_async_copy(found.at[part], found_hbm.at[part], left.at[place]))
        results[-1].start()
    for result in results:
        result.wait()


def forward_kernel(
    slot_ref, returned_ref, key_w_hbm, value_w_hbm, x_ref, c_ref, gain_ref,
    key_ref, value_ref, stat_ref, near_ref, far_ref, key_w_ref, value_w_ref,
    slots, returned_f32, memory_f32, memory_ref, came, slots_came,
):
    tokens, width = x_ref.shape
    to_smem = pltpu.make_async_copy(slot_ref, slots, slots_came)
    to_smem.start()
    chunk = 256
    weights = []
    for place in range(width // chunk):
        columns = pl.ds(place * chunk, chunk)
        for which, (source, weight) in enumerate(((key_w_hbm, key_w_ref), (value_w_hbm, value_w_ref))):
            weights.append(
                pltpu.make_async_copy(source.at[:, columns], weight.at[:, columns], came.at[2 * place + which])
            )
            weights[-1].start()
    lookups = slot_ref.shape[0]
    returned_f32[...] = returned_ref[...].astype(F32)
    to_smem.wait()
    for look in range(lookups):
        for token in range(tokens):
            target = look * tokens + token
            memory_f32[target : target + 1, :] = returned_f32[pl.ds(slots[look, token], 1), :]
    for look in range(lookups):
        memory_ref[:, look * LANES : (look + 1) * LANES] = memory_f32[look * tokens : (look + 1) * tokens, :].astype(BF16)
    memory = memory_ref[...]
    xx = kk = vv = xk = cv = jnp.zeros((tokens, LANES), F32)
    for start in range(0, width, chunk):
        weights[start // chunk * 2].wait()
        weights[start // chunk * 2 + 1].wait()
        key_ref[:, start : start + chunk] = jnp.dot(
            memory, key_w_ref[:, start : start + chunk], preferred_element_type=F32
        )
        value_ref[:, start : start + chunk] = jnp.dot(
            memory, value_w_ref[:, start : start + chunk], preferred_element_type=F32
        )
        for part in range(start, start + chunk, LANES):
            cols = slice(part, part + LANES)
            x = x_ref[:, cols].astype(F32)
            key = key_ref[:, cols]
            value = value_ref[:, cols]
            xx += x * x
            kk += key * key
            vv += value * value
            xk += x * key * gain_ref[:, cols]
            cv += c_ref[:, cols].astype(F32) * value
    xx, kk, vv, xk, cv = (jnp.sum(s, axis=-1, keepdims=True) for s in (xx, kk, vv, xk, cv))
    hidden_scale = lax.rsqrt(xx / width + EPSILON)
    key_scale = lax.rsqrt(kk / width + EPSILON)
    gate = jax.nn.sigmoid(hidden_scale * key_scale * xk / math.sqrt(width))
    conv_scale = lax.rsqrt(gate * gate * vv / width + EPSILON)
    for place, stat in enumerate((hidden_scale, key_scale, gate, conv_scale, xk, cv)):
        stat_ref[:, place : place + 1] = stat
    scaled = gate * conv_scale
    first = value_ref[:8, :] * scaled[:8]
    last = value_ref[tokens - 8 :, :] * scaled[tokens - 8 :]
    odd = lax.axis_index("seq") % 2 == 1
    near_ref[...] = jnp.where(odd, first, last)
    far_ref[...] = jnp.where(odd, last, first)


def slope_of(conv_out):
    sigmoid = jax.nn.sigmoid(conv_out)
    return sigmoid * (1.0 + conv_out * (1.0 - sigmoid))


def alone_kernel(
    key_ref, value_ref, stat_ref, x_ref, c_ref, gain_ref, taps_ref, key_w_ref,
    conv_ref, back_ref, uv_ref, key_part_ref,
    conv_in, conv_grad, key_grad,
):
    tokens, width = value_ref.shape
    taps = taps_ref.shape[0]
    wide = (tokens, LANES)
    hidden_scale, key_scale, gate, conv_scale, xk = (stat_ref[:, i : i + 1] for i in range(5))
    scaled = jnp.broadcast_to(gate * conv_scale, wide)
    both = jnp.broadcast_to(hidden_scale * key_scale, wide)
    from_key = jnp.broadcast_to(hidden_scale * key_scale * key_scale * key_scale * xk / width, wide)
    for start in range(0, width, LANES):
        cols = slice(start, start + LANES)
        key_grad[:, cols] = (
            both * gain_ref[:, cols] * x_ref[:, cols].astype(F32) - from_key * key_ref[:, cols]
        ).astype(BF16)
    span = 256
    for start in range(0, key_part_ref.shape[1], span):
        rows = slice(start, start + span)
        key_part_ref[:, rows] = lax.dot_general(
            key_grad[...], key_w_ref[rows, :], NT, preferred_element_type=F32
        )
    conv_in[0:8, :] = jnp.zeros((8, LANES), F32)
    conv_grad[tokens:, :] = jnp.zeros((8, LANES), F32)
    uv_ref[...] = jnp.zeros(wide, F32)
    for start in range(0, width, LANES):
        cols = slice(start, start + LANES)
        conv_in[8:, :] = value_ref[:, cols] * scaled
        conv_out = taps_ref[0:1, cols] * conv_in[8:, :]
        for tap in range(1, taps):
            conv_out += taps_ref[tap : tap + 1, cols] * conv_in[8 - tap : 8 + tokens - tap, :]
        conv_ref[:, cols] = conv_out
        conv_grad[0:tokens, :] = c_ref[:, cols].astype(F32) * slope_of(conv_out)
        u = taps_ref[0:1, cols] * conv_grad[0:tokens, :]
        for tap in range(1, taps):
            u += taps_ref[tap : tap + 1, cols] * conv_grad[tap : tap + tokens, :]
        back_ref[:, cols] = u
        uv_ref[...] += u * value_ref[:, cols]


def finish_kernel(
    slot_ref, value_ref, stat_ref, c_ref, taps_ref, conv_ref, back_ref, uv_ref, key_part_ref,
    near_ref, far_ref, later_c_ref, value_w_ref,
    coef_hbm, head_hbm, grads_hbm,
    coef_ref, head_ref, sent, rim, rim_grad, rim_back, rim_uv, value_grad, memory_grad, slots, packed, left, slot_of, slots_came,
):
    to_smem = pltpu.make_async_copy(slot_ref, slot_of, slots_came)
    to_smem.start()
    tokens, width = value_ref.shape
    lookups = slot_ref.shape[0]
    taps = taps_ref.shape[0]
    seq = lax.axis_index("seq")
    odd = seq % 2 == 1
    has_earlier = jnp.where(seq > 0, 1.0, 0.0)
    has_later = jnp.where(seq < lax.axis_size("seq") - 1, 1.0, 0.0)
    hidden_scale, key_scale, gate, conv_scale, xk, cv = (stat_ref[:, i : i + 1] for i in range(6))
    scaled = gate * conv_scale
    last = slice(tokens - 8, tokens)
    rim_uv[...] = jnp.zeros_like(rim_uv)
    rim[8:16, :] = jnp.zeros((8, LANES), F32)
    rim_grad[0:8, :] = jnp.zeros((8, LANES), F32)
    rim_grad[16:24, :] = jnp.zeros((8, LANES), F32)
    slots[...] = jnp.zeros_like(slots)
    for start in range(0, width, LANES):
        cols = slice(start, start + LANES)
        weights = [taps_ref[tap : tap + 1, cols] for tap in range(taps)]
        alone = conv_ref[0:8, cols]
        near, far = near_ref[:, cols], far_ref[:, cols]
        rim[0:8, :] = jnp.where(odd, near, far) * has_earlier
        joined = alone
        for tap in range(1, taps):
            joined += weights[tap] * rim[8 - tap : 16 - tap, :]
        head_ref[:, cols] = joined
        rim_grad[8:16, :] = c_ref[0:16, cols].astype(F32)[:8] * (slope_of(joined) - slope_of(alone))
        u = back_ref[0:8, cols]
        for tap in range(taps):
            u += weights[tap] * rim_grad[8 + tap : 16 + tap, :]
        rim_back[0:8, cols] = u
        rim_uv[0:8, :] += u * value_ref[0:8, cols]
        rim[16:24, :] = value_ref[last, cols] * scaled[last]
        rim[24:32, :] = jnp.where(odd, far, near) * has_later
        beyond = weights[0] * rim[24:32, :]
        for tap in range(1, taps):
            beyond += weights[tap] * rim[24 - tap : 32 - tap, :]
        rim_grad[32:40, :] = later_c_ref[:, cols].astype(F32)[:8] * slope_of(beyond) * has_later
        u = back_ref[last, cols]
        rim_grad[24:32, :] = jnp.zeros((8, LANES), F32)
        for tap in range(1, taps):
            u += weights[tap] * rim_grad[24 + tap : 32 + tap, :]
        rim_back[8:16, cols] = u
        rim_uv[8:16, :] += u * value_ref[last, cols]
    uv = jnp.sum(
        jnp.concatenate([rim_uv[0:8, :], uv_ref[8 : tokens - 8, :], rim_uv[8:16, :]], axis=0), axis=-1, keepdims=True
    )
    cube = conv_scale * conv_scale * conv_scale
    gate_grad = cv + EPSILON * cube * uv
    score_grad = gate_grad * gate * (1.0 - gate) / math.sqrt(width)
    both = score_grad * hidden_scale * key_scale
    from_hidden = both * hidden_scale * hidden_scale * xk / width
    from_value = gate * gate * cube * uv / width
    coef_ref[:, 0:1] = both
    coef_ref[:, 1:2] = from_hidden
    coef_ref[:, 2:3] = gate
    small = [
        pltpu.make_async_copy(coef_ref, coef_hbm, sent.at[0]),
        pltpu.make_async_copy(head_ref, head_hbm, sent.at[1]),
    ]
    for copy in small:
        copy.start()
    wide = (tokens, LANES)
    score_w = jnp.broadcast_to(score_grad, wide)
    value_w = jnp.broadcast_to(gate * from_value, wide)
    scaled_w = jnp.broadcast_to(scaled, wide)
    gate_w = jnp.broadcast_to(gate, wide)
    for start in range(0, width, LANES):
        cols = slice(start, start + LANES)
        u = jnp.concatenate([rim_back[0:8, cols], back_ref[8 : tokens - 8, cols], rim_back[8:16, cols]], axis=0)
        value_grad[:, cols] = (
            gate_w * c_ref[:, cols].astype(F32) + scaled_w * u - value_w * value_ref[:, cols]
        ).astype(BF16)
    span = 256

    def place(looks):
        for look in looks:
            for token in range(tokens):
                slots[pl.ds(slot_of[look, token], 1), :] = memory_grad[look * tokens + token : look * tokens + token + 1, :]

    to_smem.wait()
    done = range(0)
    for start in range(0, lookups * LANES, span):
        some = lax.dot_general(
            value_grad[...], value_w_ref[start : start + span, :], NT, preferred_element_type=F32
        )
        place(done)
        done = range(start // LANES, (start + span) // LANES)
        for look in done:
            cols = slice(look * LANES, (look + 1) * LANES)
            memory_grad[look * tokens : (look + 1) * tokens, :] = (
                some[:, look * LANES - start : (look + 1) * LANES - start] + score_w * key_part_ref[:, cols]
            )
    place(done)
    pieces = left.shape[0]
    rows = slots.shape[0] // pieces
    copies = []
    for piece in range(pieces):
        part = pl.ds(piece * rows, rows)
        packed[part, :] = slots[part, :].astype(BF16)
        copies.append(pltpu.make_async_copy(packed.at[part], grads_hbm.at[part], left.at[piece]))
        copies[-1].start()
    for copy in small + copies:
        copy.wait()


def outputs_kernel(key_ref, value_ref, coef_ref, x_ref, c_ref, gain_ref, conv_ref, head_ref, mixed_ref, hidden_ref):
    tokens, width = x_ref.shape
    both, own, gate = (jnp.broadcast_to(coef_ref[:, i : i + 1], (tokens, LANES)) for i in range(3))
    for start in range(0, width, LANES):
        cols = slice(start, start + LANES)
        x = x_ref[:, cols].astype(F32)
        conv_out = jnp.concatenate([head_ref[:, cols], conv_ref[8:, cols]], axis=0)
        mixed_ref[:, cols] = (x + conv_out * jax.nn.sigmoid(conv_out) + gate * value_ref[:, cols]).astype(BF16)
        hidden_ref[:, cols] = (
            c_ref[:, cols].astype(F32) + both * gain_ref[:, cols] * key_ref[:, cols] - own * x
        ).astype(BF16)


def add_kernel(capacity, tiles_ref, arrived_ref, out_hbm, tiles, moved, left, arrived, *totals):
    to_smem = pltpu.make_async_copy(tiles_ref, tiles, moved)
    to_smem.start()
    ways = len(totals)
    devices = arrived_ref.shape[0] // capacity
    group = devices * 8 // tiles_ref.shape[0]
    for total in totals:
        total[...] = jnp.zeros_like(total)
    arrived[...] = arrived_ref[...].astype(F32)
    to_smem.wait()
    for ranks in range(0, capacity, 8):

        def one_rank(inner, carry, ranks=ranks):
            for first in range(0, devices, ways):
                rows = [
                    tiles[device // group * 8 + inner, ranks // 8 * group + device % group]
                    for device in range(first, first + ways)
                ]
                sums = [
                    totals[way][pl.ds(rows[way], 1), :] + arrived[pl.ds(inner + ranks + (first + way) * capacity, 1), :]
                    for way in range(ways)
                ]
                for way in range(ways):
                    totals[way][pl.ds(rows[way], 1), :] = sums[way]
            return carry

        lax.fori_loop(0, 8, one_rank, 0)
    pieces = left.shape[0]
    each = out_hbm.shape[0] // pieces
    copies = []
    for piece in range(pieces):
        part = pl.ds(piece * each, each)
        sums = totals[0][part, :]
        for total in totals[1:]:
            sums = sums + total[part, :]
        totals[0][part, :] = sums
        copies.append(pltpu.make_async_copy(totals[0].at[part], out_hbm.at[part], left.at[piece]))
        copies[-1].start()
    for copy in copies:
        copy.wait()


def shards(
    hidden, row_ids, table, key_weight, value_weight, hidden_gain, key_gain, conv_gain, conv_kernel, cotangent
):
    tokens, width = hidden.shape[1:]
    lookups = row_ids.shape[2]
    rows_here, row_width = table.shape
    devices = lax.axis_size(("seq", "rows"))
    capacity = 3 * tokens * lookups // devices
    places = devices * capacity
    x, c = hidden[0], cotangent[0]
    gain = (hidden_gain * key_gain)[None]
    taps = conv_kernel * conv_gain[None]
    shape = jax.ShapeDtypeStruct

    send, slot_of = pl.pallas_call(
        functools.partial(route_kernel, rows_here, capacity),
        out_shape=(shape((devices, LANES), jnp.int32), shape((lookups, tokens), jnp.int32)),
        in_specs=[VMEM],
        out_specs=(VMEM, VMEM),
        name="route",
    )(row_ids[0].T)
    asked = exchange(send)
    table_here = pl.pallas_call(
        stage_table_kernel,
        out_shape=shape((rows_here, row_width), BF16),
        in_specs=[VMEM, ANY],
        out_specs=VMEM,
        scratch_shapes=[pltpu.SemaphoreType.DMA],
        compiler_params=params(4),
        cost_estimate=pl.CostEstimate(flops=places * row_width, bytes_accessed=6 * places * row_width, transcendentals=0),
        name="stage_table",
    )(slot_of, in_hbm(table))
    groups = 4
    found, tiles = pl.pallas_call(
        functools.partial(fetch_kernel, capacity),
        out_shape=(pltpu.HBM((places, row_width), BF16), shape((8 * groups, LANES), jnp.int32)),
        in_specs=[VMEM, VMEM],
        out_specs=(ANY, VMEM),
        scratch_shapes=[
            pltpu.SMEM((8 * groups, LANES), jnp.int32),
            pltpu.VMEM((rows_here, row_width), F32),
            pltpu.VMEM((places, row_width), F32),
            pltpu.VMEM((places, row_width), BF16),
            pltpu.SemaphoreType.DMA((groups,)),
            pltpu.SemaphoreType.DMA((groups,)),
        ],
        compiler_params=params(8),
        name="fetch",
    )(asked, table_here)
    returned = exchange(found.reshape(devices, capacity, row_width)).reshape(places, row_width)
    later_c = shifted(c[:16], "seq", -1)
    key, value, stats, near, far, key_w, value_w = pl.pallas_call(
        forward_kernel,
        out_shape=(
            shape((tokens, width), F32),
            shape((tokens, width), F32),
            shape((tokens, LANES), F32),
            shape((8, width), F32),
            shape((8, width), F32),
            shape(key_weight.shape, BF16),
            shape(value_weight.shape, BF16),
        ),
        in_specs=[VMEM, VMEM, ANY, ANY, VMEM, VMEM, VMEM],
        out_specs=(VMEM,) * 7,
        scratch_shapes=[
            pltpu.SMEM((lookups, tokens), jnp.int32),
            pltpu.VMEM((places, row_width), F32),
            pltpu.VMEM((tokens * lookups, row_width), F32),
            pltpu.VMEM((tokens, lookups * row_width), BF16),
            pltpu.SemaphoreType.DMA((width // 128,)),
            pltpu.SemaphoreType.DMA,
        ],
        compiler_params=params(8),
        name="forward",
    )(slot_of, returned, in_hbm(key_weight), in_hbm(value_weight), x, c, gain)
    blocks = lax.axis_size("seq")
    near = lax.ppermute(near, "seq", [(i, i ^ 1) for i in range(blocks)])
    far = lax.ppermute(far, "seq", [(i, (i + (1 if i % 2 else -1)) % blocks) for i in range(blocks)])
    conv_out, back, uv, key_part = pl.pallas_call(
        alone_kernel,
        out_shape=(
            shape((tokens, width), F32),
            shape((tokens, width), F32),
            shape((tokens, LANES), F32),
            shape((tokens, lookups * row_width), F32),
        ),
        in_specs=[VMEM] * 8,
        out_specs=(VMEM,) * 4,
        scratch_shapes=[
            pltpu.VMEM((tokens + 8, LANES), F32),
            pltpu.VMEM((tokens + 8, LANES), F32),
            pltpu.VMEM((tokens, width), BF16),
        ],
        compiler_params=params(4),
        cost_estimate=pl.CostEstimate(
            flops=40 * tokens * width, bytes_accessed=4 * key_weight.size, transcendentals=2 * tokens * width
        ),
        name="alone",
    )(key, value, stats, x, c, gain, taps, key_w)
    coef, head, grads = pl.pallas_call(
        finish_kernel,
        out_shape=(
            pltpu.HBM((tokens, LANES), F32),
            pltpu.HBM((8, width), F32),
            pltpu.HBM((places, row_width), BF16),
        ),
        in_specs=[VMEM] * 13,
        out_specs=(ANY,) * 3,
        scratch_shapes=[
            pltpu.VMEM((tokens, LANES), F32),
            pltpu.VMEM((8, width), F32),
            pltpu.SemaphoreType.DMA((2,)),
            pltpu.VMEM((32, LANES), F32),
            pltpu.VMEM((40, LANES), F32),
            pltpu.VMEM((16, width), F32),
            pltpu.VMEM((16, LANES), F32),
            pltpu.VMEM((tokens, width), BF16),
            pltpu.VMEM((tokens * lookups, row_width), F32),
            pltpu.VMEM((places, row_width), F32),
            pltpu.VMEM((places, row_width), BF16),
            pltpu.SemaphoreType.DMA((4,)),
            pltpu.SMEM((lookups, tokens), jnp.int32),
            pltpu.SemaphoreType.DMA,
        ],
        compiler_params=params(12),
        name="finish",
    )(slot_of, value, stats, c, taps, conv_out, back, uv, key_part, near, far, later_c, value_w)
    arrived = exchange(grads.reshape(devices, capacity, row_width)).reshape(places, row_width)
    mixed, hidden_grad = pl.pallas_call(
        outputs_kernel,
        out_shape=(shape((tokens, width), BF16), shape((tokens, width), BF16)),
        in_specs=[VMEM] * 8,
        out_specs=(VMEM, VMEM),
        cost_estimate=pl.CostEstimate(
            flops=10 * tokens * width, bytes_accessed=20 * tokens * width, transcendentals=tokens * width
        ),
        name="outputs",
    )(key, value, coef, x, c, gain, conv_out, head)
    ways = 8
    table_grad = pl.pallas_call(
        functools.partial(add_kernel, capacity),
        out_shape=pltpu.HBM((rows_here, row_width), F32),
        in_specs=[VMEM, VMEM],
        out_specs=ANY,
        scratch_shapes=[
            pltpu.SMEM((8 * groups, LANES), jnp.int32),
            pltpu.SemaphoreType.DMA,
            pltpu.SemaphoreType.DMA((4,)),
            pltpu.VMEM((places, row_width), F32),
        ]
        + [pltpu.VMEM((rows_here, row_width), F32)] * ways,
        compiler_params=params(24),
        name="add",
    )(tiles, arrived)
    return (mixed[None], hidden_grad[None], table_grad)


def solution(mesh):
    seq_block = P("rows", "seq", None)
    table_block = P(("seq", "rows"), None)
    return jax.shard_map(
        shards,
        mesh=mesh,
        in_specs=(seq_block, seq_block, table_block, P(), P(), P(), P(), P(), P(), seq_block),
        out_specs=(seq_block, seq_block, table_block),
        check_vma=False,
    )
```
